32 devices in a mesh: groups: 2 (over y), seq: 16 (over z, x, core).
Axes of the slice: x: 2, y: 2, z: 4, core: 2. Of those that a mesh axis runs over, the one named last changes fastest.
Arguments:
- queries: bfloat16 [12288, 2048], P(('groups', 'seq')), parts along dimension 0, may hold values from -6 to 6
- key_vectors: bfloat16 [12288, 2048], P(('groups', 'seq')), parts along dimension 0, may hold values from -6 to 6
- value_vectors: bfloat16 [12288, 2048], P(('groups', 'seq')), parts along dimension 0, may hold values from -6 to 6
- out_cotangent: bfloat16 [12288, 2048], P(('groups', 'seq')), parts along dimension 0, may hold values from -6 to 6
- norm_gain: float32 [2048], replicated, may hold values from 0.1 to 1.9
Outputs:
- query_grad: bfloat16 [12288, 2048], P(('groups', 'seq')), parts along dimension 0
- key_grad: bfloat16 [12288, 2048], P(('groups', 'seq')), parts along dimension 0
- value_grad: bfloat16 [12288, 2048], P(('groups', 'seq')), parts along dimension 0
- gain_grad: float32 [4096], P('groups'), parts along dimension 0
The draws below stay inside these ranges and needn't reach their ends.
There are 2 independent parts, one for each index of `groups`. The reference program is written for one: setup_inputs(seed, part) draws one part's arguments, and reference() takes and returns one part's arrays. A program takes and returns all parts, laid end to end along the dimension named above; an argument that names none is the same for every part. Nothing has to cross between parts.
All inputs are finite; a program needn't handle non-finite values.
Results may differ from the reference program's by a relative error of at most 0.011.
Values may be sent and summed in bfloat16 or wider, within the bound.
No kernel may reach another device: no remote copies, remote signals or barrier semaphores. Data moves between devices by JAX's collectives and lax.ppermute only.
A program may use at most 128 MiB of HBM per device.

```python
import jax
import jax.numpy as jnp
from jax import lax

HEADS = 16
HEAD = 128
TOK_DEV = 384
SEQLEN = 6144
N_SEQ = 16


def block_scale(stream_key, dims, pieces, least, largest):
    gain, own = 1.0, jax.random.fold_in(stream_key, 6)
    for axis_at, shards_of in pieces:
        draws = jnp.exp(jax.random.uniform(jax.random.fold_in(own, axis_at), (shards_of,), jnp.float32, least / len(pieces), largest / len(pieces)))
        gain = gain * jnp.repeat(draws, dims[axis_at] // shards_of).reshape([-1 if axis == axis_at else 1 for axis in range(len(dims))])
    return gain


def normal_values(key, dims, width, bound, pieces=(), held_as=jnp.bfloat16):
    drawn = width * jax.random.normal(key, dims, jnp.float32)
    if pieces:
        drawn = drawn * block_scale(key, dims, pieces, -0.22, 0.18)
    return jnp.clip(drawn, -bound, bound).astype(held_as)


def setup_inputs(seed: int = 0, part: int = 0) -> dict:
    keys = jax.random.split(jax.random.key(seed), 6)
    own_keys = jax.random.split(jax.random.fold_in(keys[5], part), 6)
    queries = normal_values(own_keys[0], (SEQLEN, HEADS * HEAD), 1.0, 6.0, ((0, 16),))
    key_vectors = normal_values(own_keys[1], (SEQLEN, HEADS * HEAD), 1.0, 6.0, ((0, 16),))
    value_vectors = normal_values(own_keys[2], (SEQLEN, HEADS * HEAD), 1.0, 6.0, ((0, 16),))
    out_cotangent = normal_values(own_keys[3], (SEQLEN, HEADS * HEAD), 1.0, 6.0, ((0, 16),))
    norm_gain = jnp.clip(1.0 + 0.18 * jax.random.normal(keys[4], (HEADS * HEAD,), jnp.float32), 0.1, 1.9)
    return {"queries": queries, "key_vectors": key_vectors, "value_vectors": value_vectors, "out_cotangent": out_cotangent, "norm_gain": norm_gain}


norm_eps = 1e-05

def feature(x):
    return jnp.where(x > 0, x + 1.0, jnp.exp(jnp.minimum(x, 0.0)))

def slope(x):
    return jnp.where(x > 0, 1.0, jnp.exp(jnp.minimum(x, 0.0)))

def block_weights(query_map, key_map):
    rows = query_map.shape[0]
    causal = jnp.tril(jnp.ones((rows, rows), dtype=bool))
    scores = jnp.einsum('thd,shd->hts', query_map.astype(jnp.float32), key_map.astype(jnp.float32))
    return (jnp.where(causal[None], scores, 0.0).astype(jnp.bfloat16), causal)

def forward_block(query_map, key_map, value_rows, cotan, state_in, gain_rows):
    weights, causal = block_weights(query_map, key_map)
    state_low = state_in.astype(jnp.bfloat16).astype(jnp.float32)
    mixed = jnp.einsum('hts,she->the', weights.astype(jnp.float32), value_rows.astype(jnp.float32))
    mixed = mixed + jnp.einsum('thd,hde->the', query_map.astype(jnp.float32), state_low)
    rms = jnp.sqrt(lax.optimization_barrier(jnp.mean(mixed * mixed, axis=-1, keepdims=True)) + norm_eps)
    normed = mixed / rms
    cot = cotan.astype(jnp.float32)
    gain_part = lax.optimization_barrier(jnp.sum(cot * normed, axis=0))
    scaled = cot * gain_rows
    grad_mixed = ((scaled - normed * lax.optimization_barrier(jnp.mean(scaled * normed, axis=-1, keepdims=True))) / rms).astype(jnp.bfloat16)
    query_state = jnp.einsum('thd,the->hde', query_map.astype(jnp.float32), grad_mixed.astype(jnp.float32))
    return (grad_mixed, gain_part, query_state)

def backward_block(items):
    query_raw, key_raw, query_map, key_map, value_rows, grad_mixed, state_in, state_back = items
    weights, causal = block_weights(query_map, key_map)
    gm = grad_mixed.astype(jnp.float32)
    vr = value_rows.astype(jnp.float32)
    qm = query_map.astype(jnp.float32)
    km = key_map.astype(jnp.float32)
    d_scores = jnp.einsum('the,she->hts', gm, vr)
    d_weights = jnp.where(causal[None], d_scores, 0.0).astype(jnp.bfloat16).astype(jnp.float32)
    state_low = state_in.astype(jnp.bfloat16).astype(jnp.float32)
    back_low = state_back.astype(jnp.bfloat16).astype(jnp.float32)
    d_query = jnp.einsum('hts,shd->thd', d_weights, km) + jnp.einsum('the,hde->thd', gm, state_low)
    d_key = jnp.einsum('hts,thd->shd', d_weights, qm) + jnp.einsum('the,hde->thd', vr, back_low)
    d_value = jnp.einsum('hts,the->she', weights.astype(jnp.float32), gm) + jnp.einsum('thd,hde->the', km, back_low)
    query_grad = (d_query * slope(query_raw.astype(jnp.float32))).astype(jnp.bfloat16)
    key_grad = (d_key * slope(key_raw.astype(jnp.float32))).astype(jnp.bfloat16)
    return (query_grad, key_grad, d_value.astype(jnp.bfloat16))

def reference(queries, key_vectors, value_vectors, out_cotangent, norm_gain):
    shape = (N_SEQ, TOK_DEV, HEADS, HEAD)
    query_blocks = queries.reshape(shape)
    key_blocks = key_vectors.reshape(shape)
    value_blocks = value_vectors.reshape(shape)
    cot_blocks = out_cotangent.reshape(shape)
    query_map = feature(query_blocks.astype(jnp.float32)).astype(jnp.bfloat16)
    key_map = feature(key_blocks.astype(jnp.float32)).astype(jnp.bfloat16)

    def own_of(pair):
        return jnp.einsum('thd,the->hde', pair[0].astype(jnp.float32), pair[1].astype(jnp.float32))
    own = lax.map(own_of, (key_map, value_blocks))
    ahead = jnp.cumsum(own, axis=0)
    state_in = jnp.concatenate([jnp.zeros_like(own[:1]), ahead[:-1]], axis=0)
    gain_rows = norm_gain.reshape(HEADS, HEAD)

    def forward_of(items):
        return forward_block(items[0], items[1], items[2], items[3], items[4], gain_rows)
    grad_mixed, gain_parts, query_states = lax.map(forward_of, (query_map, key_map, value_blocks, cot_blocks, state_in))
    gain_grad = lax.optimization_barrier(jnp.sum(gain_parts, axis=0)).reshape(HEADS * HEAD)
    behind = jnp.cumsum(query_states[::-1], axis=0)[::-1]
    state_back = jnp.concatenate([behind[1:], jnp.zeros_like(behind[:1])], axis=0)
    query_grad, key_grad, value_grad = lax.map(backward_block, (query_blocks, key_blocks, query_map, key_map, value_blocks, grad_mixed, state_in, state_back))
    flat = (SEQLEN, HEADS * HEAD)
    return (query_grad.reshape(flat), key_grad.reshape(flat), value_grad.reshape(flat), gain_grad)
```

```python
import functools

import jax
import jax.numpy as jnp
from jax import lax
from jax.experimental import pallas as pl
from jax.experimental.pallas import tpu as pltpu
from jax.sharding import PartitionSpec as P

HEADS = 16
HEAD = 128
TILE = 128
GROUP = 2
norm_eps = 1e-05
f32 = jnp.float32
bf16 = jnp.bfloat16


def decay(x):
    return jnp.exp(jnp.minimum(x, 0.0))


def feature(x):
    return jnp.where(x > 0, x + 1.0, decay(x)).astype(bf16)


def mm(a, b):
    return lax.dot_general(a, b, (((1,), (0,)), ((), ())), preferred_element_type=f32)


def mm_nt(a, b):
    return lax.dot_general(a, b, (((1,), (1,)), ((), ())), preferred_element_type=f32)


def mm_tn(a, b):
    return lax.dot_general(a, b, (((0,), (0,)), ((), ())), preferred_element_type=f32)


def cols(head):
    return slice(head * HEAD, (head + 1) * HEAD)


def lower(rows, depth, length):
    keep = lax.broadcasted_iota(jnp.int32, (TILE, TILE), 0) >= lax.broadcasted_iota(
        jnp.int32, (TILE, TILE), 1
    )
    strips = []
    for start in range(0, length, TILE):
        strip = mm_nt(rows[start : start + TILE], depth[: start + TILE])
        last = jnp.where(keep, strip[:, start:], 0.0).astype(bf16)
        if start:
            last = jnp.concatenate([strip[:, :start].astype(bf16), last], axis=1)
        strips.append(last)
    return strips


def upper(rows, depth, length):
    keep = lax.broadcasted_iota(jnp.int32, (TILE, TILE), 0) <= lax.broadcasted_iota(
        jnp.int32, (TILE, TILE), 1
    )
    strips = []
    for start in range(0, length, TILE):
        strip = mm_nt(rows[start : start + TILE], depth[start:])
        first = jnp.where(keep, strip[:, :TILE], 0.0).astype(bf16)
        if start + TILE < length:
            first = jnp.concatenate([first, strip[:, TILE:].astype(bf16)], axis=1)
        strips.append(first)
    return strips


def state_kernel(_, key_ref, value_ref, own_ref):
    for head in range(GROUP):
        key_map = feature(key_ref[:, cols(head)].astype(f32))
        own_ref[cols(head), :] = mm_tn(key_map, value_ref[:, cols(head)]).astype(bf16)


def inner_kernel(query_ref, key_ref, value_ref, mixed_ref):
    length = query_ref.shape[0]
    for head in range(GROUP):
        at = cols(head)
        query_map = feature(query_ref[:, at].astype(f32))
        key_map = feature(key_ref[:, at].astype(f32))
        value = value_ref[:, at]
        for i, strip in enumerate(lower(query_map, key_map, length)):
            start = i * TILE
            mixed_ref[start : start + TILE, at] = mm(strip, value[: start + TILE])


def norm_kernel(_, query_ref, cotan_ref, gain_ref, state_ref, mixed_ref, *refs):
    grad_ref, own_ref, part_ref = refs[-3:]
    for head in range(GROUP):
        at = cols(head)
        query_map = feature(query_ref[:, at].astype(f32))
        mixed = mixed_ref[:, at] + mm(query_map, state_ref[at, :])
        inverse = lax.rsqrt(jnp.mean(mixed * mixed, axis=1, keepdims=True) + norm_eps)
        normed = mixed * inverse
        cotan = cotan_ref[:, at].astype(f32)
        part_ref[:, at] = jnp.sum(cotan * normed, axis=0, keepdims=True)
        scaled = cotan * gain_ref[:, at]
        along = jnp.mean(scaled * normed, axis=1, keepdims=True)
        grad = ((scaled - normed * along) * inverse).astype(bf16)
        grad_ref[:, at] = grad
        own_ref[at, :] = mm_tn(query_map, grad).astype(bf16)


def back_kernel(query_ref, key_ref, value_ref, grad_ref, state_ref, dq_ref, dk_ref, dv_ref):
    length = query_ref.shape[0]
    for head in range(GROUP):
        at = cols(head)
        query = query_ref[:, at].astype(f32)
        query_map = feature(query)
        key_map = feature(key_ref[:, at].astype(f32))
        value = value_ref[:, at]
        grad = grad_ref[:, at]
        far = mm_nt(grad, state_ref[at, :])
        slope = decay(query)
        for i, strip in enumerate(lower(grad, value, length)):
            rows = slice(i * TILE, (i + 1) * TILE)
            near = mm(strip, key_map[: (i + 1) * TILE])
            dq_ref[rows, at] = ((near + far[rows]) * slope[rows]).astype(bf16)
        for i, strip in enumerate(upper(value, grad, length)):
            rows = slice(i * TILE, (i + 1) * TILE)
            dk_ref[rows, at] = mm(strip, query_map[i * TILE :])
        for i, strip in enumerate(upper(key_map, query_map, length)):
            rows = slice(i * TILE, (i + 1) * TILE)
            dv_ref[rows, at] = mm(strip, grad[i * TILE :])


def last_kernel(_, key_ref, value_ref, back_ref, dk_ref, dv_ref, *refs):
    key_grad_ref, value_grad_ref = refs[-2:]
    for head in range(GROUP):
        at = cols(head)
        key = key_ref[:, at].astype(f32)
        back = back_ref[at, :]
        far = mm_nt(value_ref[:, at], back)
        key_grad_ref[:, at] = ((dk_ref[:, at] + far) * decay(key)).astype(bf16)
        value_grad_ref[:, at] = (dv_ref[:, at] + mm(feature(key), back)).astype(bf16)


def call(kernel, half, ins, outs, steps, kept=()):
    picks = half is not None

    def spec(kind, shape):
        offset = picks and not (
            (kind == "state" and shape[0] == steps * GROUP * HEAD)
            or (kind != "state" and shape[1] == steps * GROUP * HEAD)
        )

        def place(j, *refs):
            j = refs[0][0] * steps + j if offset else j
            return (j, 0) if kind == "state" else (0, j)

        block = (GROUP * HEAD, HEAD) if kind == "state" else (shape[0], GROUP * HEAD)
        return pl.BlockSpec(block, place)

    out_shapes = [jax.ShapeDtypeStruct(shape, dtype) for _, shape, dtype in outs]
    grid_spec = pltpu.PrefetchScalarGridSpec(
        num_scalar_prefetch=int(picks),
        grid=(steps,),
        in_specs=[spec(kind, a.shape) for kind, a in ins]
        + [pl.BlockSpec(memory_space=pl.ANY)] * len(kept),
        out_specs=[spec(kind, shape) for kind, shape, _ in outs],
    )
    first = int(picks) + len(ins)
    return pl.pallas_call(
        kernel,
        out_shape=out_shapes,
        grid_spec=grid_spec,
        input_output_aliases={first + i: i for i in range(len(kept))},
        compiler_params=pltpu.CompilerParams(vmem_limit_bytes=40 << 20),
    )(*([half] if picks else []), *[a for _, a in ins], *kept)


def permute(value, pairs):
    return lax.ppermute(value, "seq", pairs)


def sum_low(*terms):
    return functools.reduce(lambda a, b: a + b, [t.astype(f32) for t in terms]).astype(bf16)


def part(value, index, rows):
    return lax.dynamic_slice_in_dim(value, index * rows, rows, 0)


class Scan:
    def __init__(self, shards, reverse):
        index = lax.axis_index("seq")
        self.shards = shards
        self.sign = -1 if reverse else 1
        self.core = (1 - index % 2) if reverse else index % 2
        self.chip = (1 - index // 2 % 2) if reverse else index // 2 % 2
        self.swap_core = [(i, i ^ 1) for i in range(shards)]
        self.swap_chip = [(i, i ^ 2) for i in range(shards)]

    def shift(self, value, fours):
        step = 4 * fours * self.sign
        pairs = [(i, i + step) for i in range(self.shards) if 0 <= i + step < self.shards]
        return permute(value, pairs)

    def before(self, total):
        count = self.shards // 4
        if count <= 4:
            return [self.shift(total, k) for k in range(count - 1, 0, -1)]
        running, step = self.shift(total, 1), 1
        while step < count - 1:
            running = sum_low(running, self.shift(running, step))
            step *= 2
        return [running]

    def start(self, theirs):
        return permute(theirs, self.swap_core)

    def totals(self, mine, got):
        rows = mine.shape[0] // 2
        self.mine, self.got = mine, got
        send = sum_low(part(mine, 1 - self.chip, rows), part(got, 1 - self.chip, rows))
        self.near = sum_low(part(mine, self.chip, rows), part(got, self.chip, rows))
        self.other = permute(send, self.swap_chip)
        return sum_low(self.near, self.other)

    def finish(self, earlier):
        base = functools.reduce(lambda a, b: a + b, [e.astype(f32) for e in earlier])
        first = jnp.where(self.chip == 0, self.near, self.other).astype(f32)
        low, high = base.astype(bf16), (base + first).astype(bf16)
        keep = jnp.where(self.chip == 0, low, high)
        back = permute(jnp.where(self.chip == 0, high, low), self.swap_chip)
        half = jnp.where(
            self.chip == 0, jnp.concatenate([keep, back]), jnp.concatenate([back, keep])
        )
        first = jnp.where(self.core == 0, self.mine, self.got)
        low, high = half, sum_low(half, first)
        mine = jnp.where(self.core == 0, low, high)
        theirs = permute(jnp.where(self.core == 0, high, low), self.swap_core)
        return mine, theirs


def on_device(queries, key_vectors, value_vectors, out_cotangent, norm_gain):
    length, width = queries.shape
    shards = lax.axis_size("seq")
    steps = HEADS // GROUP
    core = lax.axis_index("seq") % 2
    mine = core.astype(jnp.int32).reshape(1)
    theirs = 1 - mine
    gain = norm_gain.reshape(1, width)
    half_state = ("state", (width // 2, HEAD), bf16)

    def own_of(half):
        return call(
            state_kernel, half, [("tok", key_vectors), ("tok", value_vectors)], [half_state], steps // 2
        )[0]

    fore = Scan(shards, False)
    sent = own_of(theirs)
    got = fore.start(sent)
    total = fore.totals(own_of(mine), got)
    earlier = fore.before(total)
    (inner_queries, _) = lax.optimization_barrier((queries, total))
    (inner,) = call(
        inner_kernel,
        None,
        [("tok", inner_queries), ("tok", key_vectors), ("tok", value_vectors)],
        [("tok", (length, width), f32)],
        steps,
    )
    state_mine, state_theirs = fore.finish(earlier)

    def norm_of(half, state, kept):
        return call(
            norm_kernel,
            half,
            [
                ("tok", queries),
                ("tok", out_cotangent),
                ("row", gain),
                ("state", state),
                ("tok", inner),
            ],
            [("tok", (length, width), bf16), half_state, ("row", (1, width // 2), f32)],
            steps // 2,
            kept,
        )

    aft = Scan(shards, True)
    grad, sent, part_mine = norm_of(mine, state_mine, ())
    got = aft.start(sent)
    grad, own, part_theirs = norm_of(theirs, state_theirs, (grad,))
    gain_part = jnp.where(
        core == 0,
        jnp.concatenate([part_mine, part_theirs], 1),
        jnp.concatenate([part_theirs, part_mine], 1),
    )
    gain_total = jnp.sum(lax.all_gather(gain_part.reshape(HEADS, HEAD), "seq"), axis=0)
    total = aft.totals(own, got)
    later = aft.before(total)
    state = jnp.where(
        core == 0,
        jnp.concatenate([state_mine, state_theirs]),
        jnp.concatenate([state_theirs, state_mine]),
    )
    (back_grad, _) = lax.optimization_barrier((grad, total))
    query_grad, key_inner, value_inner = call(
        back_kernel,
        None,
        [
            ("tok", queries),
            ("tok", key_vectors),
            ("tok", value_vectors),
            ("tok", back_grad),
            ("state", state),
        ],
        [("tok", (length, width), bf16), ("tok", (length, width), f32), ("tok", (length, width), f32)],
        steps,
    )
    back_theirs, back_mine = aft.finish(later)

    def last_of(half, back, kept):
        return call(
            last_kernel,
            half,
            [
                ("tok", key_vectors),
                ("tok", value_vectors),
                ("state", back),
                ("tok", key_inner),
                ("tok", value_inner),
            ],
            [("tok", (length, width), bf16)] * 2,
            steps // 2,
            kept,
        )

    grads = last_of(theirs, back_theirs, ())
    key_grad, value_grad = last_of(mine, back_mine, tuple(grads))
    return query_grad, key_grad, value_grad, gain_total.reshape(width)


def solution(mesh):
    tokens = P(("groups", "seq"), None)
    return jax.shard_map(
        on_device,
        mesh=mesh,
        in_specs=(tokens, tokens, tokens, tokens, P()),
        out_specs=(tokens, tokens, tokens, P("groups")),
        check_vma=False,
    )
```

```python
import functools

import jax
import jax.numpy as jnp
from jax import lax
from jax.experimental import pallas as pl
from jax.experimental.pallas import tpu as pltpu
from jax.sharding import PartitionSpec as P

HEADS = 16
HEAD = 128
TILE = 128
GROUP = 2
norm_eps = 1e-05
f32 = jnp.float32
bf16 = jnp.bfloat16


def decay(x):
    return jnp.exp(jnp.minimum(x, 0.0))


def feature(x):
    return jnp.where(x > 0, x + 1.0, decay(x)).astype(bf16)


def mm(a, b):
    return lax.dot_general(a, b, (((1,), (0,)), ((), ())), preferred_element_type=f32)


def mm_nt(a, b):
    return lax.dot_general(a, b, (((1,), (1,)), ((), ())), preferred_element_type=f32)


def mm_tn(a, b):
    return lax.dot_general(a, b, (((0,), (0,)), ((), ())), preferred_element_type=f32)


def cols(head):
    return slice(head * HEAD, (head + 1) * HEAD)


def lower(rows, depth, length):
    keep = lax.broadcasted_iota(jnp.int32, (TILE, TILE), 0) >= lax.broadcasted_iota(
        jnp.int32, (TILE, TILE), 1
    )
    strips = []
    for start in range(0, length, TILE):
        strip = mm_nt(rows[start : start + TILE], depth[: start + TILE])
        last = jnp.where(keep, strip[:, start:], 0.0).astype(bf16)
        if start:
            last = jnp.concatenate([strip[:, :start].astype(bf16), last], axis=1)
        strips.append(last)
    return strips


def upper(rows, depth, length):
    keep = lax.broadcasted_iota(jnp.int32, (TILE, TILE), 0) <= lax.broadcasted_iota(
        jnp.int32, (TILE, TILE), 1
    )
    strips = []
    for start in range(0, length, TILE):
        strip = mm_nt(rows[start : start + TILE], depth[start:])
        first = jnp.where(keep, strip[:, :TILE], 0.0).astype(bf16)
        if start + TILE < length:
            first = jnp.concatenate([first, strip[:, TILE:].astype(bf16)], axis=1)
        strips.append(first)
    return strips


def state_kernel(_, key_ref, value_ref, own_ref):
    for head in range(GROUP):
        key_map = feature(key_ref[:, cols(head)].astype(f32))
        own_ref[cols(head), :] = mm_tn(key_map, value_ref[:, cols(head)]).astype(bf16)


def inner_kernel(query_ref, key_ref, value_ref, mixed_ref):
    length = query_ref.shape[0]
    for head in range(GROUP):
        at = cols(head)
        query_map = feature(query_ref[:, at].astype(f32))
        key_map = feature(key_ref[:, at].astype(f32))
        value = value_ref[:, at]
        for i, strip in enumerate(lower(query_map, key_map, length)):
            start = i * TILE
            mixed_ref[start : start + TILE, at] = mm(strip, value[: start + TILE])


def norm_kernel(_, query_ref, cotan_ref, gain_ref, state_ref, mixed_ref, *refs):
    grad_ref, own_ref, part_ref = refs[-3:]
    for head in range(GROUP):
        at = cols(head)
        query_map = feature(query_ref[:, at].astype(f32))
        mixed = mixed_ref[:, at] + mm(query_map, state_ref[at, :])
        inverse = lax.rsqrt(jnp.mean(mixed * mixed, axis=1, keepdims=True) + norm_eps)
        normed = mixed * inverse
        cotan = cotan_ref[:, at].astype(f32)
        part_ref[:, at] = jnp.sum(cotan * normed, axis=0, keepdims=True)
        scaled = cotan * gain_ref[:, at]
        along = jnp.mean(scaled * normed, axis=1, keepdims=True)
        grad = ((scaled - normed * along) * inverse).astype(bf16)
        grad_ref[:, at] = grad
        own_ref[at, :] = mm_tn(query_map, grad).astype(bf16)


def back_kernel(query_ref, key_ref, value_ref, grad_ref, state_ref, dq_ref, dk_ref, dv_ref):
    length = query_ref.shape[0]
    for head in range(GROUP):
        at = cols(head)
        query = query_ref[:, at].astype(f32)
        query_map = feature(query)
        key_map = feature(key_ref[:, at].astype(f32))
        value = value_ref[:, at]
        grad = grad_ref[:, at]
        far = mm_nt(grad, state_ref[at, :])
        slope = decay(query)
        for i, strip in enumerate(lower(grad, value, length)):
            rows = slice(i * TILE, (i + 1) * TILE)
            near = mm(strip, key_map[: (i + 1) * TILE])
            dq_ref[rows, at] = ((near + far[rows]) * slope[rows]).astype(bf16)
        for i, strip in enumerate(upper(value, grad, length)):
            rows = slice(i * TILE, (i + 1) * TILE)
            dk_ref[rows, at] = mm(strip, query_map[i * TILE :])
        for i, strip in enumerate(upper(key_map, query_map, length)):
            rows = slice(i * TILE, (i + 1) * TILE)
            dv_ref[rows, at] = mm(strip, grad[i * TILE :])


def last_kernel(_, key_ref, value_ref, back_ref, dk_ref, dv_ref, *refs):
    key_grad_ref, value_grad_ref = refs[-2:]
    for head in range(GROUP):
        at = cols(head)
        key = key_ref[:, at].astype(f32)
        back = back_ref[at, :]
        far = mm_nt(value_ref[:, at], back)
        key_grad_ref[:, at] = ((dk_ref[:, at] + far) * decay(key)).astype(bf16)
        value_grad_ref[:, at] = (dv_ref[:, at] + mm(feature(key), back)).astype(bf16)


def call(kernel, half, ins, outs, steps, kept=()):
    picks = half is not None

    def spec(kind, shape):
        offset = picks and not (
            (kind == "state" and shape[0] == steps * GROUP * HEAD)
            or (kind != "state" and shape[1] == steps * GROUP * HEAD)
        )

        def place(j, *refs):
            j = refs[0][0] * steps + j if offset else j
            return (j, 0) if kind == "state" else (0, j)

        block = (GROUP * HEAD, HEAD) if kind == "state" else (shape[0], GROUP * HEAD)
        return pl.BlockSpec(block, place)

    out_shapes = [jax.ShapeDtypeStruct(shape, dtype) for _, shape, dtype in outs]
    grid_spec = pltpu.PrefetchScalarGridSpec(
        num_scalar_prefetch=int(picks),
        grid=(steps,),
        in_specs=[spec(kind, a.shape) for kind, a in ins]
        + [pl.BlockSpec(memory_space=pl.ANY)] * len(kept),
        out_specs=[spec(kind, shape) for kind, shape, _ in outs],
    )
    first = int(picks) + len(ins)
    return pl.pallas_call(
        kernel,
        out_shape=out_shapes,
        grid_spec=grid_spec,
        input_output_aliases={first + i: i for i in range(len(kept))},
        compiler_params=pltpu.CompilerParams(vmem_limit_bytes=16 << 20),
    )(*([half] if picks else []), *[a for _, a in ins], *kept)


def permute(value, pairs):
    return lax.ppermute(value, "seq", pairs)


def sum_low(*terms):
    return functools.reduce(lambda a, b: a + b, [t.astype(f32) for t in terms]).astype(bf16)


def part(value, index, rows):
    return lax.dynamic_slice_in_dim(value, index * rows, rows, 0)


class Scan:
    def __init__(self, shards, reverse):
        index = lax.axis_index("seq")
        self.shards = shards
        self.sign = -1 if reverse else 1
        self.core = (1 - index % 2) if reverse else index % 2
        self.chip = (1 - index // 2 % 2) if reverse else index // 2 % 2
        self.swap_core = [(i, i ^ 1) for i in range(shards)]
        self.swap_chip = [(i, i ^ 2) for i in range(shards)]

    def shift(self, value, fours):
        step = 4 * fours * self.sign
        pairs = [(i, i + step) for i in range(self.shards) if 0 <= i + step < self.shards]
        return permute(value, pairs)

    def before(self, total):
        count = self.shards // 4
        if count <= 4:
            return [self.shift(total, k) for k in range(count - 1, 0, -1)]
        running, step = self.shift(total, 1), 1
        while step < count - 1:
            running = sum_low(running, self.shift(running, step))
            step *= 2
        return [running]

    def start(self, theirs):
        return permute(theirs, self.swap_core)

    def totals(self, mine, got):
        rows = mine.shape[0] // 2
        self.mine, self.got = mine, got
        send = sum_low(part(mine, 1 - self.chip, rows), part(got, 1 - self.chip, rows))
        self.near = sum_low(part(mine, self.chip, rows), part(got, self.chip, rows))
        self.other = permute(send, self.swap_chip)
        return sum_low(self.near, self.other)

    def finish(self, earlier):
        base = functools.reduce(lambda a, b: a + b, [e.astype(f32) for e in earlier])
        first = jnp.where(self.chip == 0, self.near, self.other).astype(f32)
        low, high = base.astype(bf16), (base + first).astype(bf16)
        keep = jnp.where(self.chip == 0, low, high)
        back = permute(jnp.where(self.chip == 0, high, low), self.swap_chip)
        half = jnp.where(
            self.chip == 0, jnp.concatenate([keep, back]), jnp.concatenate([back, keep])
        )
        first = jnp.where(self.core == 0, self.mine, self.got)
        low, high = half, sum_low(half, first)
        mine = jnp.where(self.core == 0, low, high)
        theirs = permute(jnp.where(self.core == 0, high, low), self.swap_core)
        return mine, theirs


class Butterfly:
    def __init__(self, value, shards):
        self.value, self.level, self.shards = value, 0, shards

    def round(self):
        if 1 << self.level < self.shards:
            pairs = [(i, i ^ 1 << self.level) for i in range(self.shards)]
            self.value = self.value + permute(self.value, pairs)
            self.level += 1

    def beside(self, value):
        self.round()
        value, self.value = lax.optimization_barrier((value, self.value))
        return value

    def total(self):
        while 1 << self.level < self.shards:
            self.round()
        return self.value


def on_device(queries, key_vectors, value_vectors, out_cotangent, norm_gain):
    queries, key_vectors, value_vectors, out_cotangent = (
        pltpu.with_memory_space_constraint(a, pltpu.HBM)
        for a in (queries, key_vectors, value_vectors, out_cotangent)
    )
    length, width = queries.shape
    shards = lax.axis_size("seq")
    steps = HEADS // GROUP
    core = lax.axis_index("seq") % 2
    mine = core.astype(jnp.int32).reshape(1)
    theirs = 1 - mine
    gain = norm_gain.reshape(1, width)
    half_state = ("state", (width // 2, HEAD), bf16)

    def own_of(half):
        return call(
            state_kernel, half, [("tok", key_vectors), ("tok", value_vectors)], [half_state], steps // 2
        )[0]

    fore = Scan(shards, False)
    sent = own_of(theirs)
    got = fore.start(sent)
    total = fore.totals(own_of(mine), got)
    earlier = fore.before(total)
    (inner_queries, _) = lax.optimization_barrier((queries, total))
    (inner,) = call(
        inner_kernel,
        None,
        [("tok", inner_queries), ("tok", key_vectors), ("tok", value_vectors)],
        [("tok", (length, width), f32)],
        steps,
    )
    state_mine, state_theirs = fore.finish(earlier)

    def norm_of(half, state, kept):
        return call(
            norm_kernel,
            half,
            [
                ("tok", queries),
                ("tok", out_cotangent),
                ("row", gain),
                ("state", state),
                ("tok", inner),
            ],
            [("tok", (length, width), bf16), half_state, ("row", (1, width // 2), f32)],
            steps // 2,
            kept,
        )

    aft = Scan(shards, True)
    grad, sent, part_mine = norm_of(mine, state_mine, ())
    got = aft.start(sent)
    grad, own, part_theirs = norm_of(theirs, state_theirs, (grad,))
    gain_part = jnp.where(
        core == 0,
        jnp.concatenate([part_mine, part_theirs], 1),
        jnp.concatenate([part_theirs, part_mine], 1),
    )
    gains = Butterfly(gain_part.reshape(HEADS, HEAD), shards)
    total = gains.beside(aft.totals(own, got))
    later = aft.before(total)
    state = jnp.where(
        core == 0,
        jnp.concatenate([state_mine, state_theirs]),
        jnp.concatenate([state_theirs, state_mine]),
    )
    (back_grad, _) = lax.optimization_barrier((grad, total))
    query_grad, key_inner, value_inner = call(
        back_kernel,
        None,
        [
            ("tok", queries),
            ("tok", key_vectors),
            ("tok", value_vectors),
            ("tok", back_grad),
            ("state", state),
        ],
        [("tok", (length, width), bf16), ("tok", (length, width), f32), ("tok", (length, width), f32)],
        steps,
    )
    later = gains.beside(lax.optimization_barrier((*later, key_inner))[:-1])
    back_theirs, back_mine = aft.finish(later)
    back_theirs = gains.beside(back_theirs)

    def last_of(half, back, kept):
        return call(
            last_kernel,
            half,
            [
                ("tok", key_vectors),
                ("tok", value_vectors),
                ("state", back),
                ("tok", key_inner),
                ("tok", value_inner),
            ],
            [("tok", (length, width), bf16)] * 2,
            steps // 2,
            kept,
        )

    grads = last_of(theirs, back_theirs, ())
    key_grad, value_grad = last_of(mine, back_mine, tuple(grads))
    return query_grad, key_grad, value_grad, gains.total().reshape(width)


def solution(mesh):
    tokens = P(("groups", "seq"), None)
    return jax.shard_map(
        on_device,
        mesh=mesh,
        in_specs=(tokens, tokens, tokens, tokens, P()),
        out_specs=(tokens, tokens, tokens, P("groups")),
        check_vma=False,
    )
```

```python
import functools

import jax
import jax.numpy as jnp
from jax import lax
from jax.experimental import pallas as pl
from jax.experimental.pallas import tpu as pltpu
from jax.sharding import PartitionSpec as P

HEADS = 16
HEAD = 128
TILE = 128
QUARTER = HEADS // 4
SPAN = QUARTER * HEAD
EXTRA = 16
norm_eps = 1e-05
f32 = jnp.float32
bf16 = jnp.bfloat16

VMEM = pl.BlockSpec(memory_space=pltpu.VMEM)
SMEM = pl.BlockSpec(memory_space=pltpu.SMEM)
HBM = pl.BlockSpec(memory_space=pltpu.HBM)


def decay(x):
    return jnp.exp(jnp.minimum(x, 0.0))


def feature(x):
    return jnp.where(x > 0, x + 1.0, decay(x)).astype(bf16)


def mm(a, b):
    return lax.dot_general(a, b, (((1,), (0,)), ((), ())), preferred_element_type=f32)


def mm_nt(a, b):
    return lax.dot_general(a, b, (((1,), (1,)), ((), ())), preferred_element_type=f32)


def mm_tn(a, b):
    return lax.dot_general(a, b, (((0,), (0,)), ((), ())), preferred_element_type=f32)


def own(head):
    return slice(head * HEAD, (head + 1) * HEAD)


def span(where):
    return pl.ds(pl.multiple_of((2 * where[0] + where[1]) * SPAN, SPAN), SPAN)


def place(where, head):
    start = (2 * where[0] + where[1]) * SPAN + head * HEAD
    return pl.ds(pl.multiple_of(start, HEAD), HEAD)


def lower(rows, depth, length):
    keep = lax.broadcasted_iota(jnp.int32, (TILE, TILE), 0) >= lax.broadcasted_iota(
        jnp.int32, (TILE, TILE), 1
    )
    strips = []
    for start in range(0, length, TILE):
        strip = mm_nt(rows[start : start + TILE], depth[: start + TILE])
        last = jnp.where(keep, strip[:, start:], 0.0).astype(bf16)
        if start:
            last = jnp.concatenate([strip[:, :start].astype(bf16), last], axis=1)
        strips.append(last)
    return strips


def upper(rows, depth, length):
    keep = lax.broadcasted_iota(jnp.int32, (TILE, TILE), 0) <= lax.broadcasted_iota(
        jnp.int32, (TILE, TILE), 1
    )
    strips = []
    for start in range(0, length, TILE):
        strip = mm_nt(rows[start : start + TILE], depth[start:])
        first = jnp.where(keep, strip[:, :TILE], 0.0).astype(bf16)
        if start + TILE < length:
            first = jnp.concatenate([first, strip[:, TILE:].astype(bf16)], axis=1)
        strips.append(first)
    return strips


def finish(copies):
    for copy in copies:
        copy.wait()


def state(ins, outs):
    (key_ref, value_ref), (own_ref,) = ins, outs
    for head in range(QUARTER):
        key_map = feature(key_ref[:, own(head)].astype(f32))
        own_ref[own(head), :] = mm_tn(key_map, value_ref[:, own(head)]).astype(own_ref.dtype)


def inner(ins, outs):
    (query_ref, key_ref, value_ref), (mixed_ref,) = ins, outs
    length = query_ref.shape[0]
    for head in range(QUARTER):
        query_map = feature(query_ref[:, own(head)].astype(f32))
        key_map = feature(key_ref[:, own(head)].astype(f32))
        value = value_ref[:, own(head)]
        for i, strip in enumerate(lower(query_map, key_map, length)):
            start = i * TILE
            mixed_ref[start : start + TILE, own(head)] = mm(strip, value[: start + TILE])


def loading_kernel(body, first, *refs):
    body_ins, body_outs, loads = body[1:]
    where, refs = refs[:loads], refs[loads:]
    ins, refs = refs[:body_ins], refs[body_ins:]
    sources, refs = refs[:loads], refs[loads:]
    outs, refs = refs[:body_outs], refs[body_outs:]
    targets, sems = refs[:loads], refs[-1]
    copies = [
        pltpu.make_async_copy(source.at[:, span(at)], target, sems.at[i])
        for i, (at, source, target) in enumerate(zip(where, sources, targets, strict=True))
    ]
    for copy in copies:
        copy.start()
    finish(copies[:first])
    body[0]((*targets[:first], *ins), outs)
    finish(copies[first:])


def plain_kernel(body, count, *refs):
    body(refs[:count], refs[count:])


def norm_kernel(where, query_ref, cotan_ref, gain_ref, state_ref, mixed_ref, grad_ref, own_ref):
    own_ref[SPAN:, :] = jnp.zeros_like(own_ref[SPAN:, :])
    for head in range(QUARTER):
        query_map = feature(query_ref[:, own(head)].astype(f32))
        mixed = mixed_ref[:, own(head)] + mm(query_map, state_ref[own(head), :])
        inverse = lax.rsqrt(jnp.mean(mixed * mixed, axis=1, keepdims=True) + norm_eps)
        normed = mixed * inverse
        cotan = cotan_ref[:, own(head)].astype(f32)
        part = jnp.sum(cotan * normed, axis=0, keepdims=True)
        own_ref[SPAN + head : SPAN + head + 1, :] = part.astype(own_ref.dtype)
        scaled = cotan * gain_ref[:, place(where, head)]
        along = jnp.mean(scaled * normed, axis=1, keepdims=True)
        grad = ((scaled - normed * along) * inverse).astype(bf16)
        grad_ref[:, own(head)] = grad
        own_ref[own(head), :] = mm_tn(query_map, grad).astype(own_ref.dtype)


def back_kernel(where, query_ref, key_ref, value_ref, grad_ref, state_ref, *refs):
    dk_ref, dv_ref, dq_hbm, dq_ref, sems = refs[-5:]
    length = query_ref.shape[0]
    copies = []
    for head in range(QUARTER):
        query = query_ref[:, own(head)].astype(f32)
        query_map = feature(query)
        key_map = feature(key_ref[:, own(head)].astype(f32))
        value = value_ref[:, own(head)]
        grad = grad_ref[:, own(head)]
        far = mm_nt(grad, state_ref[own(head), :])
        slope = decay(query)
        for i, strip in enumerate(lower(grad, value, length)):
            rows = slice(i * TILE, (i + 1) * TILE)
            near = mm(strip, key_map[: (i + 1) * TILE])
            dq_ref[rows, own(head)] = ((near + far[rows]) * slope[rows]).astype(bf16)
        copies.append(
            pltpu.make_async_copy(
                dq_ref.at[:, own(head)], dq_hbm.at[:, place(where, head)], sems.at[head]
            )
        )
        copies[-1].start()
        for i, strip in enumerate(upper(value, grad, length)):
            rows = slice(i * TILE, (i + 1) * TILE)
            dk_ref[rows, own(head)] = mm(strip, query_map[i * TILE :])
        for i, strip in enumerate(upper(key_map, query_map, length)):
            rows = slice(i * TILE, (i + 1) * TILE)
            dv_ref[rows, own(head)] = mm(strip, grad[i * TILE :])
    finish(copies)


def last_kernel(where, key_ref, value_ref, back_ref, dk_ref, dv_ref, so_far_ref, *refs):
    key_hbm, value_hbm, gain_ref, key_grad_ref, value_grad_ref, sems = refs[-6:]
    copies = []
    gain_ref[...] = so_far_ref[...]
    gains = back_ref[SPAN:, :].astype(f32)
    for head in range(QUARTER):
        gain_ref[:, place(where, head)] = gains[head : head + 1, :]
        key = key_ref[:, own(head)].astype(f32)
        back = back_ref[own(head), :]
        far = mm_nt(value_ref[:, own(head)], back)
        key_grad_ref[:, own(head)] = ((dk_ref[:, own(head)] + far) * decay(key)).astype(bf16)
        value_grad = dv_ref[:, own(head)] + mm(feature(key), back)
        value_grad_ref[:, own(head)] = value_grad.astype(bf16)
        for i, (held, whole) in enumerate(((key_grad_ref, key_hbm), (value_grad_ref, value_hbm))):
            copies.append(
                pltpu.make_async_copy(
                    held.at[:, own(head)], whole.at[:, place(where, head)], sems.at[i, head]
                )
            )
            copies[-1].start()
    finish(copies)


def call(kernel, ins, outs, scratch=(), kept=()):
    return pl.pallas_call(
        kernel,
        out_shape=[jax.ShapeDtypeStruct(shape, dtype) for shape, dtype, _ in outs],
        in_specs=[spec for _, spec in ins] + [spec for _, spec, _ in kept],
        out_specs=[spec for _, _, spec in outs],
        scratch_shapes=list(scratch),
        input_output_aliases={len(ins) + i: out for i, (_, _, out) in enumerate(kept)},
        compiler_params=pltpu.CompilerParams(vmem_limit_bytes=12 << 20),
        cost_estimate=pl.CostEstimate(flops=1024, bytes_accessed=1024, transcendentals=0),
    )(*[a for a, _ in ins], *[a for a, _, _ in kept])


def permute(value, pairs):
    return lax.ppermute(value, "seq", pairs)


def add(*terms):
    return functools.reduce(lambda a, b: a + b, [t.astype(f32) for t in terms])


def when(flag, wanted, value):
    value = value.astype(f32)
    return jnp.where(flag, value, 0.0) if wanted else jnp.where(flag, 0.0, value)


def after(value, *done):
    leaves, tree = jax.tree.flatten(value)
    held = lax.optimization_barrier((*leaves, *done))
    return jax.tree.unflatten(tree, held[: len(leaves)])


class Scan:
    def __init__(self, shards, reverse, odd_core, odd_chip, ends):
        self.shards = shards
        self.sign = -1 if reverse else 1
        self.second = not reverse
        self.odd_core, self.odd_chip, self.ends = odd_core, odd_chip, ends

    def swap_core(self, value):
        return permute(value, [(i, i ^ 1) for i in range(self.shards)])

    def swap_chip(self, value):
        return permute(value, [(i, i ^ 2) for i in range(self.shards)])

    def shift(self, value, fours):
        step = 4 * fours * self.sign
        if value.shape[0] > SPAN:
            moved = permute(value, [(i, (i + step) % self.shards) for i in range(self.shards)])
            rows = lax.broadcasted_iota(jnp.int32, value.shape, 0)
            return jnp.where(self.ends[fours] | (rows >= SPAN), moved, 0)
        pairs = [(i, i + step) for i in range(self.shards) if 0 <= i + step < self.shards]
        return permute(value, pairs)

    def early(self, mine, got):
        self.early_mine, self.early_got = mine, got
        send = add(mine, got).astype(bf16)
        self.other = self.swap_chip(send)
        return send

    def late(self, mine, got):
        self.late_mine, self.late_got = mine, got
        self.near = add(mine, got)

    def before(self):
        total = add(self.near, self.other).astype(bf16)
        self.total = total
        count = self.shards // 4
        if count <= 4:
            return total, [self.shift(total, k) for k in range(1, count)]
        running, step = self.shift(total, 1), 1
        while step < count:
            running = add(running, self.shift(running, step)).astype(bf16)
            step *= 2
        return total, [running]

    def alone(self, value, wanted):
        rows = lax.broadcasted_iota(jnp.int32, value.shape, 0)
        return jnp.where((rows >= SPAN) if wanted else (rows < SPAN), value, 0)

    def state(self, base, mine, got):
        if base.shape[0] > SPAN:
            mine, got = self.alone(mine, False), self.alone(got, False)
        here = add(base, when(self.odd_core, self.second, got)).astype(bf16)
        there = add(base, when(self.odd_core, not self.second, mine)).astype(bf16)
        return here, self.swap_core(there)

    def late_state(self, earlier):
        base = add(*earlier)
        near, other = self.near, self.other
        if base.shape[0] > SPAN:
            if self.shards // 4 <= 4:
                base = base + self.alone(self.total, True).astype(f32)
            near, other = self.alone(near, False), self.alone(other, False)
        send = add(base, when(self.odd_chip, not self.second, near)).astype(bf16)
        self.back = self.swap_chip(send)
        base = add(base, when(self.odd_chip, self.second, other))
        return self.state(base, self.late_mine, self.late_got)

    def early_state(self):
        return self.state(self.back, self.early_mine, self.early_got)


def on_device(queries, key_vectors, value_vectors, out_cotangent, norm_gain):
    queries, key_vectors, value_vectors, out_cotangent = (
        pltpu.with_memory_space_constraint(a, pltpu.HBM)
        for a in (queries, key_vectors, value_vectors, out_cotangent)
    )
    length, width = queries.shape
    shards = lax.axis_size("seq")
    index = lax.axis_index("seq").astype(jnp.int32)
    core, chip, four = index % 2, index // 2 % 2, index // 4
    gain = norm_gain.reshape(1, width)
    where = {
        (a, b): jnp.stack([1 - core if a else core, 1 - chip if b else chip])
        for a in (0, 1)
        for b in (0, 1)
    }
    count = shards // 4
    ends = {k: four + k < count for k in range(1, count)}
    where, odd_core, odd_chip, ends = after((where, core == 1, chip == 1, ends))
    state_low = ((SPAN, HEAD), bf16, VMEM)
    state_wide = ((SPAN, HEAD), f32, VMEM)
    sums_low = ((SPAN + EXTRA, HEAD), bf16, VMEM)
    sums_wide = ((SPAN + EXTRA, HEAD), f32, VMEM)
    wide = ((length, SPAN), f32, VMEM)
    low = ((length, SPAN), bf16, VMEM)
    whole = ((length, width), bf16, HBM)
    row = ((1, width), f32, VMEM)
    held = lambda *arrays: [(a, VMEM) for a in arrays]
    sems = lambda *shape: pltpu.SemaphoreType.DMA(shape)
    wholes = {"q": queries, "k": key_vectors, "v": value_vectors, "c": out_cotangent}
    tile = {}

    def loading(body, ins, outs, fetch, first=0):
        kernel = functools.partial(
            loading_kernel, (body, len(ins), len(outs), len(fetch)), first
        )
        result = call(
            kernel,
            [(where[which], SMEM) for _, which in fetch]
            + held(*ins)
            + [(wholes[name], HBM) for name, _ in fetch],
            outs + [low] * len(fetch),
            [sems(len(fetch))],
        )
        for key, value in zip(fetch, result[len(outs) :], strict=True):
            tile[key] = value
        return result[: len(outs)]

    def tiles(names, which):
        return [tile[name, which] for name in names]

    fore = Scan(shards, False, odd_core, odd_chip, ends)
    (sent,) = loading(
        state, [], [state_low], [("k", (1, 1)), ("v", (1, 1)), ("k", (0, 1)), ("v", (0, 1))], 2
    )
    got = fore.swap_core(sent)
    (mine,) = loading(
        state, after(tiles("kv", (0, 1)), sent), [state_wide], [("k", (1, 0)), ("v", (1, 0))]
    )
    send = fore.early(mine, got)
    (sent,) = loading(
        state, after(tiles("kv", (1, 0)), send), [state_low], [("k", (0, 0)), ("v", (0, 0))]
    )
    got = fore.swap_core(sent)
    (mine,) = loading(
        state, after(tiles("kv", (0, 0)), sent), [state_wide], [("q", (0, 0)), ("q", (1, 0))]
    )
    fore.late(mine, got)

    mixed = {}
    (mixed[0, 0],) = loading(
        inner, tiles("qkv", (0, 0)), [wide], [("q", (0, 1)), ("q", (1, 1))]
    )
    fore.near = after(fore.near, mixed[0, 0])
    total, earlier = fore.before()
    (mixed[1, 0],) = loading(
        inner, after(tiles("qkv", (1, 0)), total), [wide], [("c", (0, 0)), ("c", (1, 0))]
    )
    (mixed[0, 1],) = loading(
        inner, after(tiles("qkv", (0, 1)), mixed[1, 0]), [wide], [("c", (0, 1)), ("c", (1, 1))]
    )
    (mixed[1, 1],) = call(
        functools.partial(plain_kernel, inner, 3),
        held(*after(tiles("qkv", (1, 1)), mixed[0, 1])),
        [wide],
    )
    earlier = after(earlier, mixed[1, 1])

    grads, seen = {}, {}
    aft = Scan(shards, True, odd_core, odd_chip, ends)

    def norm(which, state, kind, *done):
        query, cotan = tiles("qc", which)
        (cotan,) = after([cotan], *done) if done else [cotan]
        ins = [(where[which], SMEM)] + held(query, cotan, gain, state, mixed[which])
        return call(norm_kernel, ins, [low, kind])

    seen[0, 0], seen[1, 0] = fore.late_state(earlier)
    grads[0, 0], sent = norm((0, 0), seen[0, 0], sums_low)
    got = aft.swap_core(sent)
    grads[1, 0], mine = norm((1, 0), seen[1, 0], sums_wide)
    send = aft.early(mine, got)
    fore.back = after(fore.back, send)
    seen[0, 1], seen[1, 1] = fore.early_state()
    grads[0, 1], sent = norm((0, 1), seen[0, 1], sums_low, send)
    got = aft.swap_core(sent)
    grads[1, 1], mine = norm((1, 1), seen[1, 1], sums_wide)
    aft.late(mine, got)
    total, later = aft.before()

    inner_grads = {}
    query_grad = None

    def back(which, query_grad, *done):
        grad = after(grads[which], *done)
        return call(
            back_kernel,
            [(where[which], SMEM)] + held(*tiles("qkv", which), grad, seen[which]),
            [wide, wide, whole],
            [pltpu.VMEM((length, SPAN), bf16), sems(QUARTER)],
            [] if query_grad is None else [(query_grad, HBM, 2)],
        )

    done = total
    for which in ((1, 1), (0, 1), (1, 0)):
        *inner_grads[which], query_grad = back(which, query_grad, done)
        done = inner_grads[which][0]
    later = after(later, done)

    def last(which, back, outs):
        so_far = outs[2] if outs else gain
        ins = [(where[which], SMEM)]
        ins += held(*tiles("kv", which), back, *inner_grads[which], so_far)
        scratch = [pltpu.VMEM((length, SPAN), bf16)] * 2 + [sems(2, QUARTER)]
        kept = [(a, HBM, i) for i, a in enumerate(outs[:2])]
        return call(last_kernel, ins, [whole, whole, row], scratch, kept)

    here, there = aft.late_state(later)
    outs = last((1, 1), here, ())
    *inner_grads[0, 0], query_grad = back((0, 0), query_grad, outs[2])
    inner_grads[0, 1][0] = after(inner_grads[0, 1][0], inner_grads[0, 0][0])
    outs = last((0, 1), there, outs)
    aft.back = after(aft.back, outs[2])
    here, there = aft.early_state()
    outs = last((1, 0), here, outs)
    key_grad, value_grad, gain_grad = last((0, 0), there, outs)
    return query_grad, key_grad, value_grad, gain_grad.reshape(width)


def solution(mesh):
    tokens = P(("groups", "seq"), None)
    return jax.shard_map(
        on_device,
        mesh=mesh,
        in_specs=(tokens, tokens, tokens, tokens, P()),
        out_specs=(tokens, tokens, tokens, P("groups")),
        check_vma=False,
    )
```

```python
import functools

import jax
import jax.numpy as jnp
from jax import lax
from jax.experimental import pallas as pl
from jax.experimental.pallas import tpu as pltpu
from jax.sharding import PartitionSpec as P

HEADS = 16
HEAD = 128
TILE = 128
QUARTER = HEADS // 4
SPAN = QUARTER * HEAD
WORK, LIGHT = 2_000_000_000, 300_000_000
PIECES = 2
EXTRA = 16
norm_eps = 1e-05
f32 = jnp.float32
bf16 = jnp.bfloat16

VMEM = pl.BlockSpec(memory_space=pltpu.VMEM)
SMEM = pl.BlockSpec(memory_space=pltpu.SMEM)
HBM = pl.BlockSpec(memory_space=pltpu.HBM)


def decay(x):
    return jnp.exp(jnp.minimum(x, 0.0))


def feature(x):
    return jnp.where(x > 0, x + 1.0, decay(x)).astype(bf16)


def mm(a, b):
    return lax.dot_general(a, b, (((1,), (0,)), ((), ())), preferred_element_type=f32)


def mm_nt(a, b):
    return lax.dot_general(a, b, (((1,), (1,)), ((), ())), preferred_element_type=f32)


def mm_tn(a, b):
    return lax.dot_general(a, b, (((0,), (0,)), ((), ())), preferred_element_type=f32)


def own(head):
    return slice(head * HEAD, (head + 1) * HEAD)


def span(where):
    return pl.ds(pl.multiple_of((2 * where[0] + where[1]) * SPAN, SPAN), SPAN)


def place(where, head):
    start = (2 * where[0] + where[1]) * SPAN + head * HEAD
    return pl.ds(pl.multiple_of(start, HEAD), HEAD)


def lower(rows, depth, length):
    keep = lax.broadcasted_iota(jnp.int32, (TILE, TILE), 0) >= lax.broadcasted_iota(
        jnp.int32, (TILE, TILE), 1
    )
    strips = []
    for start in range(0, length, TILE):
        strip = mm_nt(rows[start : start + TILE], depth[: start + TILE])
        last = jnp.where(keep, strip[:, start:], 0.0).astype(bf16)
        if start:
            last = jnp.concatenate([strip[:, :start].astype(bf16), last], axis=1)
        strips.append(last)
    return strips


def upper(rows, depth, length):
    keep = lax.broadcasted_iota(jnp.int32, (TILE, TILE), 0) <= lax.broadcasted_iota(
        jnp.int32, (TILE, TILE), 1
    )
    strips = []
    for start in range(0, length, TILE):
        strip = mm_nt(rows[start : start + TILE], depth[start:])
        first = jnp.where(keep, strip[:, :TILE], 0.0).astype(bf16)
        if start + TILE < length:
            first = jnp.concatenate([first, strip[:, TILE:].astype(bf16)], axis=1)
        strips.append(first)
    return strips


def finish(copies):
    for copy in copies:
        copy.wait()


def state(key_ref, value_ref, own_ref):
    for head in range(QUARTER):
        key_map = feature(key_ref[:, own(head)].astype(f32))
        own_ref[own(head), :] = mm_tn(key_map, value_ref[:, own(head)]).astype(own_ref.dtype)


def inner(query_ref, key_ref, value_ref, mixed_ref):
    length = query_ref.shape[0]
    for head in range(QUARTER):
        query_map = feature(query_ref[:, own(head)].astype(f32))
        key_map = feature(key_ref[:, own(head)].astype(f32))
        value = value_ref[:, own(head)]
        for i, strip in enumerate(lower(query_map, key_map, length)):
            start = i * TILE
            mixed_ref[start : start + TILE, own(head)] = mm(strip, value[: start + TILE])


def chunked(source, target, sem, pieces):
    rows = source.shape[0] // pieces
    return [
        pltpu.make_async_copy(
            source.at[pl.ds(i * rows, rows)], target.at[pl.ds(i * rows, rows)], sem.at[i]
        )
        for i in range(pieces)
    ]


def moving_kernel(body, counts, first, *refs):
    loads, store_to, body_ins, body_outs, wholes, scratch, named = counts
    stores = len(store_to)
    refs = list(refs)

    def take(number):
        taken = refs[:number]
        del refs[:number]
        return taken

    load_at, store_at = take(loads), take(stores)
    ins, sources, ready = take(body_ins), take(loads), take(stores)
    take(wholes)
    outs, targets, results = take(body_outs), take(loads), take(named)
    rest, (sems,) = take(scratch), take(1)
    copies = []
    for i, (at, source, target) in enumerate(zip(load_at, sources, targets, strict=True)):
        copies.append(chunked(source.at[:, span(at)], target, sems.at[i], PIECES))
    for i, (at, source, to) in enumerate(zip(store_at, ready, store_to, strict=True)):
        target = results[to].at[:, span(at)]
        copies.append(chunked(source, target, sems.at[loads + i], PIECES))
    for copy in copies:
        for piece in copy:
            piece.start()
    for copy in copies[:first]:
        finish(copy)
    body(*targets[:first], *ins, *outs, *results, *rest)
    for copy in copies[first:]:
        finish(copy)


def norm_kernel(where, query_ref, cotan_ref, gain_ref, state_ref, mixed_ref, grad_ref, own_ref):
    own_ref[SPAN:, :] = jnp.zeros_like(own_ref[SPAN:, :])
    for head in range(QUARTER):
        query_map = feature(query_ref[:, own(head)].astype(f32))
        mixed = mixed_ref[:, own(head)] + mm(query_map, state_ref[own(head), :])
        inverse = lax.rsqrt(jnp.mean(mixed * mixed, axis=1, keepdims=True) + norm_eps)
        normed = mixed * inverse
        cotan = cotan_ref[:, own(head)].astype(f32)
        part = jnp.sum(cotan * normed, axis=0, keepdims=True)
        own_ref[SPAN + head : SPAN + head + 1, :] = part.astype(own_ref.dtype)
        scaled = cotan * gain_ref[:, place(where, head)]
        along = jnp.mean(scaled * normed, axis=1, keepdims=True)
        grad = ((scaled - normed * along) * inverse).astype(bf16)
        grad_ref[:, own(head)] = grad
        own_ref[own(head), :] = mm_tn(query_map, grad).astype(own_ref.dtype)


def back(query_ref, key_ref, value_ref, grad_ref, state_ref, dk_ref, dv_ref, dq_ref, *_):
    length = query_ref.shape[0]
    for head in range(QUARTER):
        query = query_ref[:, own(head)].astype(f32)
        query_map = feature(query)
        key_map = feature(key_ref[:, own(head)].astype(f32))
        value = value_ref[:, own(head)]
        grad = grad_ref[:, own(head)]
        far = mm_nt(grad, state_ref[own(head), :])
        slope = decay(query)
        for i, strip in enumerate(lower(grad, value, length)):
            rows = slice(i * TILE, (i + 1) * TILE)
            near = mm(strip, key_map[: (i + 1) * TILE])
            dq_ref[rows, own(head)] = ((near + far[rows]) * slope[rows]).astype(bf16)
        for i, strip in enumerate(upper(value, grad, length)):
            rows = slice(i * TILE, (i + 1) * TILE)
            dk_ref[rows, own(head)] = mm(strip, query_map[i * TILE :])
        for i, strip in enumerate(upper(key_map, query_map, length)):
            rows = slice(i * TILE, (i + 1) * TILE)
            dv_ref[rows, own(head)] = mm(strip, grad[i * TILE :])


def last_head(head, key_ref, value_ref, back_ref, dk_ref, dv_ref, key_grad_ref, value_grad_ref):
    key = key_ref[:, own(head)].astype(f32)
    back = back_ref[own(head), :]
    far = mm_nt(value_ref[:, own(head)], back)
    key_grad_ref[:, own(head)] = ((dk_ref[:, own(head)] + far) * decay(key)).astype(bf16)
    value_grad = dv_ref[:, own(head)] + mm(feature(key), back)
    value_grad_ref[:, own(head)] = value_grad.astype(bf16)


def last(key_ref, value_ref, back_ref, dk_ref, dv_ref, key_grad_ref, value_grad_ref, *_):
    for head in range(QUARTER):
        last_head(
            head, key_ref, value_ref, back_ref, dk_ref, dv_ref, key_grad_ref, value_grad_ref
        )


def very_last(*refs):
    wheres, refs = refs[:4], refs[4:]
    key_ref, value_ref, dk_ref, dv_ref, *backs = refs[:8]
    gain_ref, key_hbm, value_hbm, key_grad_ref, value_grad_ref, sems = refs[8:]
    for where, back_ref in zip(wheres, backs, strict=True):
        gains = back_ref[SPAN:, :].astype(f32)
        for head in range(QUARTER):
            gain_ref[:, place(where, head)] = gains[head : head + 1, :]
    copies = []
    for head in range(QUARTER):
        last_head(
            head, key_ref, value_ref, backs[0], dk_ref, dv_ref, key_grad_ref, value_grad_ref
        )
        for i, (held, whole) in enumerate(((key_grad_ref, key_hbm), (value_grad_ref, value_hbm))):
            copies.append(
                pltpu.make_async_copy(
                    held.at[:, own(head)], whole.at[:, place(wheres[0], head)], sems.at[i, head]
                )
            )
            copies[-1].start()
    finish(copies)


def call(kernel, ins, outs, scratch=(), kept=(), flops=WORK):
    return pl.pallas_call(
        kernel,
        out_shape=[jax.ShapeDtypeStruct(shape, dtype) for shape, dtype, _ in outs],
        in_specs=[spec for _, spec in ins] + [spec for _, spec, _ in kept],
        out_specs=[spec for _, _, spec in outs],
        scratch_shapes=list(scratch),
        input_output_aliases={len(ins) + i: out for i, (_, _, out) in enumerate(kept)},
        compiler_params=pltpu.CompilerParams(vmem_limit_bytes=12 << 20),
        cost_estimate=pl.CostEstimate(flops=flops, bytes_accessed=4 << 20, transcendentals=0),
    )(*[a for a, _ in ins], *[a for a, _, _ in kept])


def permute(value, pairs):
    return lax.ppermute(value, "seq", pairs)


def add(*terms):
    return functools.reduce(lambda a, b: a + b, [t.astype(f32) for t in terms])


def when(flag, wanted, value):
    value = value.astype(f32)
    return jnp.where(flag, value, 0.0) if wanted else jnp.where(flag, 0.0, value)


def after(value, *done):
    leaves, tree = jax.tree.flatten(value)
    held = lax.optimization_barrier((*leaves, *done))
    return jax.tree.unflatten(tree, held[: len(leaves)])


class Scan:
    def __init__(self, shards, reverse, odd_core, odd_chip, bits):
        self.shards = shards
        self.sign = -1 if reverse else 1
        self.second = not reverse
        self.odd_core, self.odd_chip, self.bits = odd_core, odd_chip, bits

    def swap_core(self, value):
        return permute(value, [(i, i ^ 1) for i in range(self.shards)])

    def swap_chip(self, value):
        return permute(value, [(i, i ^ 2) for i in range(self.shards)])

    def early(self, mine, got):
        self.early_mine, self.early_got = mine, got
        send = add(mine, got).astype(bf16)
        self.other = self.swap_chip(send)
        return send

    def late(self, mine, got):
        self.late_mine, self.late_got = mine, got
        self.near = add(mine, got)

    def open(self):
        self.total = add(self.near, self.other).astype(bf16)
        self.base = 0.0
        return self.total

    def exchange(self, level):
        step = 4 << level
        return permute(self.total, [(i, i ^ step) for i in range(self.shards)])

    def absorb(self, level, other):
        self.base = self.base + when(self.bits[level], self.second, other)
        self.total = add(self.total, other).astype(bf16)
        return self.total

    def alone(self, value, wanted):
        rows = lax.broadcasted_iota(jnp.int32, value.shape, 0)
        return jnp.where((rows >= SPAN) if wanted else (rows < SPAN), value, 0)

    def state(self, base, mine, got):
        if base.shape[0] > SPAN:
            mine, got = self.alone(mine, False), self.alone(got, False)
        here = add(base, when(self.odd_core, self.second, got)).astype(bf16)
        there = add(base, when(self.odd_core, not self.second, mine)).astype(bf16)
        return here, self.swap_core(there)

    def late_state(self):
        base, near, other = self.base, self.near, self.other
        if base.shape[0] > SPAN:
            base = self.alone(base, False) + self.alone(self.total, True).astype(f32)
            near, other = self.alone(near, False), self.alone(other, False)
        send = add(base, when(self.odd_chip, not self.second, near)).astype(bf16)
        self.back = self.swap_chip(send)
        base = add(base, when(self.odd_chip, self.second, other))
        return self.state(base, self.late_mine, self.late_got)

    def early_state(self):
        return self.state(self.back, self.early_mine, self.early_got)


def on_device(queries, key_vectors, value_vectors, out_cotangent, norm_gain):
    queries, key_vectors, value_vectors, out_cotangent = (
        pltpu.with_memory_space_constraint(a, pltpu.HBM)
        for a in (queries, key_vectors, value_vectors, out_cotangent)
    )
    length, width = queries.shape
    shards = lax.axis_size("seq")
    index = lax.axis_index("seq").astype(jnp.int32)
    core, chip, four = index % 2, index // 2 % 2, index // 4
    gain = norm_gain.reshape(1, width)
    where = {
        (a, b): jnp.stack([1 - core if a else core, 1 - chip if b else chip])
        for a in (0, 1)
        for b in (0, 1)
    }
    levels = range((shards // 4 - 1).bit_length())
    bits = [four // (1 << level) % 2 == 1 for level in levels]
    where, odd_core, odd_chip, bits = after((where, core == 1, chip == 1, bits))
    state_low = ((SPAN, HEAD), bf16, VMEM)
    state_wide = ((SPAN, HEAD), f32, VMEM)
    sums_low = ((SPAN + EXTRA, HEAD), bf16, VMEM)
    sums_wide = ((SPAN + EXTRA, HEAD), f32, VMEM)
    wide = ((length, SPAN), f32, VMEM)
    low = ((length, SPAN), bf16, VMEM)
    whole = ((length, width), bf16, HBM)
    row = ((1, width), f32, VMEM)
    held = lambda *arrays: [(a, VMEM) for a in arrays]
    sems = lambda *shape: pltpu.SemaphoreType.DMA(shape)
    wholes = {"q": queries, "k": key_vectors, "v": value_vectors, "c": out_cotangent}
    tile, results = {}, {}

    def moving(body, ins, outs, fetch=(), first=0, put=(), scratch=(), flops=WORK):
        names = list(dict.fromkeys(name for _, _, name in put))
        old = [(name, results[name]) for name in names if name in results]
        store_to = tuple(names.index(name) for _, _, name in put)
        counts = (len(fetch), store_to, len(ins), len(outs), len(old), len(scratch), len(names))
        result = call(
            functools.partial(moving_kernel, body, counts, first),
            [(where[which], SMEM) for _, which in fetch]
            + [(where[which], SMEM) for which, _, _ in put]
            + ins
            + [(wholes[name], HBM) for name, _ in fetch]
            + held(*[a for _, a, _ in put]),
            outs + [low] * len(fetch) + [whole] * len(names),
            [*scratch, sems(max(1, len(fetch) + len(put)), PIECES)],
            [(a, HBM, len(outs) + len(fetch) + names.index(name)) for name, a in old],
            flops,
        )
        for key, value in zip(fetch, result[len(outs) : len(outs) + len(fetch)], strict=True):
            tile[key] = value
        for name, value in zip(names, result[len(outs) + len(fetch) :], strict=True):
            results[name] = value
        return result[: len(outs)]

    def loading(body, ins, outs, fetch=(), first=0):
        return moving(body, held(*ins), outs, fetch, first)

    def tiles(names, which):
        return [tile[name, which] for name in names]

    every = [(1, 1), (0, 1), (1, 0), (0, 0)]
    fore = Scan(shards, False, odd_core, odd_chip, bits)
    (sent,) = loading(state, [], [state_low], [(name, w) for w in every for name in "kv"], 2)
    got = fore.swap_core(sent)
    (mine,) = loading(state, after(tiles("kv", (0, 1)), sent), [state_wide])
    send = fore.early(mine, got)
    (sent,) = loading(state, after(tiles("kv", (1, 0)), send), [state_low])
    got = fore.swap_core(sent)
    (mine,) = loading(
        state, after(tiles("kv", (0, 0)), sent), [state_wide], [("q", w) for w in every]
    )
    fore.late(mine, got)

    mixed = {}
    (mixed[0, 0],) = loading(inner, tiles("qkv", (0, 0)), [wide])
    fore.near = after(fore.near, mixed[0, 0])
    done = fore.open()
    plan = {0: [(1, 0)], 1: [(0, 1), (1, 1)]}
    fetched = {(1, 0): [("c", w) for w in every]}
    for level in levels:
        moved = fore.exchange(level)
        for which in plan.get(level, []):
            (done,) = loading(
                inner, after(tiles("qkv", which), done), [wide], fetched.get(which, [])
            )
            mixed[which] = done
        done = fore.absorb(level, after(moved, done))

    grads, seen = {}, {}
    aft = Scan(shards, True, odd_core, odd_chip, bits)

    def norm(which, state, kind, *done):
        query, cotan = tiles("qc", which)
        (cotan,) = after([cotan], *done) if done else [cotan]
        ins = [(where[which], SMEM)] + held(query, cotan, gain, state, mixed[which])
        return call(norm_kernel, ins, [low, kind])

    seen[0, 0], seen[1, 0] = fore.late_state()
    grads[0, 0], sent = norm((0, 0), seen[0, 0], sums_low)
    got = aft.swap_core(sent)
    grads[1, 0], mine = norm((1, 0), seen[1, 0], sums_wide)
    send = aft.early(mine, got)
    fore.back = after(fore.back, send)
    seen[0, 1], seen[1, 1] = fore.early_state()
    grads[0, 1], sent = norm((0, 1), seen[0, 1], sums_low, send)
    got = aft.swap_core(sent)
    grads[1, 1], mine = norm((1, 1), seen[1, 1], sums_wide)
    aft.late(mine, got)

    inner_grads, ready = {}, []

    def back_of(which, done, flops=WORK):
        grad = after(grads[which], done)
        *inner_grads[which], query_grad = moving(
            back, held(*tiles("qkv", which), grad, seen[which]), [wide, wide, low], flops=flops
        )
        ready.append((which, query_grad, "query"))
        return inner_grads[which][0]

    done = aft.open()
    plan = {0: [(1, 1)], 1: [(0, 1), (1, 0)]}
    for level in levels:
        moved = aft.exchange(level)
        for which in plan.get(level, []):
            done = back_of(which, done)
        done = aft.absorb(level, after(moved, done))

    def last_of(which, back_state):
        put = [ready.pop(0) for _ in range(len(ready))]
        key_grad, value_grad = moving(
            last,
            held(*tiles("kv", which), back_state, *inner_grads[which]),
            [low, low],
            put=put,
            flops=LIGHT,
        )
        ready.extend([(which, key_grad, "key"), (which, value_grad, "value")])
        return key_grad

    backs = {}
    backs[1, 1], backs[0, 1] = aft.late_state()
    done = last_of((1, 1), backs[1, 1])
    done = back_of((0, 0), done, LIGHT)
    inner_grads[0, 1][0] = after(inner_grads[0, 1][0], done)
    done = last_of((0, 1), backs[0, 1])
    aft.back = after(aft.back, done)
    backs[1, 0], backs[0, 0] = aft.early_state()
    last_of((1, 0), backs[1, 0])
    order = ((0, 0), (1, 0), (0, 1), (1, 1))
    (gain_grad,) = moving(
        very_last,
        [(where[which], SMEM) for which in order]
        + held(*tiles("kv", (0, 0)), *inner_grads[0, 0], *[backs[which] for which in order]),
        [row],
        put=list(ready),
        scratch=[pltpu.VMEM((length, SPAN), bf16)] * 2 + [sems(2, QUARTER)],
    )
    return results["query"], results["key"], results["value"], gain_grad.reshape(width)


def solution(mesh):
    tokens = P(("groups", "seq"), None)
    return jax.shard_map(
        on_device,
        mesh=mesh,
        in_specs=(tokens, tokens, tokens, tokens, P()),
        out_specs=(tokens, tokens, tokens, P("groups")),
        check_vma=False,
    )
```

```python
import functools

import jax
import jax.numpy as jnp
from jax import lax
from jax.experimental import pallas as pl
from jax.experimental.pallas import tpu as pltpu
from jax.sharding import PartitionSpec as P

HEADS = 16
HEAD = 128
TILE = 128
QUARTER = HEADS // 4
SPAN = QUARTER * HEAD
WORK, LIGHT = 2_000_000_000, 300_000_000
PIECES = 2
EXTRA = 16
norm_eps = 1e-05
f32 = jnp.float32
bf16 = jnp.bfloat16

VMEM = pl.BlockSpec(memory_space=pltpu.VMEM)
SMEM = pl.BlockSpec(memory_space=pltpu.SMEM)
HBM = pl.BlockSpec(memory_space=pltpu.HBM)


def decay(x):
    return jnp.exp(jnp.minimum(x, 0.0))


def feature(x):
    return jnp.where(x > 0, x + 1.0, decay(x)).astype(bf16)


def mm(a, b):
    return lax.dot_general(a, b, (((1,), (0,)), ((), ())), preferred_element_type=f32)


def mm_nt(a, b):
    return lax.dot_general(a, b, (((1,), (1,)), ((), ())), preferred_element_type=f32)


def mm_tn(a, b):
    return lax.dot_general(a, b, (((0,), (0,)), ((), ())), preferred_element_type=f32)


def own(head):
    return slice(head * HEAD, (head + 1) * HEAD)


class Quarter:
    def __init__(self, index_ref, which):
        self.index_ref, self.which = index_ref, which

    def __getitem__(self, axis):
        bit = (self.index_ref[0] >> axis) & 1
        return 1 - bit if self.which[axis] else bit


def span(where):
    return pl.ds(pl.multiple_of((2 * where[0] + where[1]) * SPAN, SPAN), SPAN)


def place(where, head):
    start = (2 * where[0] + where[1]) * SPAN + head * HEAD
    return pl.ds(pl.multiple_of(start, HEAD), HEAD)


def lower(rows, depth, length):
    keep = lax.broadcasted_iota(jnp.int32, (TILE, TILE), 0) >= lax.broadcasted_iota(
        jnp.int32, (TILE, TILE), 1
    )
    strips = []
    for start in range(0, length, TILE):
        strip = mm_nt(rows[start : start + TILE], depth[: start + TILE])
        last = jnp.where(keep, strip[:, start:], 0.0).astype(bf16)
        if start:
            last = jnp.concatenate([strip[:, :start].astype(bf16), last], axis=1)
        strips.append(last)
    return strips


def finish(copies):
    for copy in copies:
        copy.wait()


def state(key_ref, value_ref, own_ref):
    for head in range(QUARTER):
        key_map = feature(key_ref[:, own(head)].astype(f32))
        own_ref[own(head), :] = mm_tn(key_map, value_ref[:, own(head)]).astype(own_ref.dtype)


def inner(query_ref, key_ref, value_ref, mixed_ref):
    length = query_ref.shape[0]
    for head in range(QUARTER):
        query_map = feature(query_ref[:, own(head)].astype(f32))
        key_map = feature(key_ref[:, own(head)].astype(f32))
        value = value_ref[:, own(head)]
        for i, strip in enumerate(lower(query_map, key_map, length)):
            start = i * TILE
            mixed_ref[start : start + TILE, own(head)] = mm(strip, value[: start + TILE])


def chunked(source, target, sem, pieces):
    rows = source.shape[0] // pieces
    return [
        pltpu.make_async_copy(
            source.at[pl.ds(i * rows, rows)], target.at[pl.ds(i * rows, rows)], sem.at[i]
        )
        for i in range(pieces)
    ]


def moving_kernel(body, counts, first, *refs):
    load_at, store_at, store_to, body_ins, body_outs, wholes, scratch, named = counts
    loads, stores = len(load_at), len(store_to)
    refs = list(refs)

    def take(number):
        taken = refs[:number]
        del refs[:number]
        return taken

    (index_ref,) = take(1)
    load_at = [Quarter(index_ref, which) for which in load_at]
    store_at = [Quarter(index_ref, which) for which in store_at]
    ins, sources, ready = take(body_ins), take(loads), take(stores)
    take(wholes)
    outs, targets, results = take(body_outs), take(loads), take(named)
    rest, (sems,) = take(scratch), take(1)
    copies = []
    for i, (at, source, target) in enumerate(zip(load_at, sources, targets, strict=True)):
        copies.append(chunked(source.at[:, span(at)], target, sems.at[i], PIECES))
    for i, (at, source, to) in enumerate(zip(store_at, ready, store_to, strict=True)):
        target = results[to].at[:, span(at)]
        copies.append(chunked(source, target, sems.at[loads + i], PIECES))
    for copy in copies:
        for piece in copy:
            piece.start()
    for copy in copies[:first]:
        finish(copy)
    body(*targets[:first], *ins, *outs, *results, *rest)
    for copy in copies[first:]:
        finish(copy)


def norm_kernel(which, index_ref, query_ref, cotan_ref, gain_ref, state_ref, mixed_ref, grad_ref, own_ref):
    where = Quarter(index_ref, which)
    own_ref[SPAN:, :] = jnp.zeros_like(own_ref[SPAN:, :])
    for head in range(QUARTER):
        query_map = feature(query_ref[:, own(head)].astype(f32))
        mixed = mixed_ref[:, own(head)] + mm(query_map, state_ref[own(head), :])
        inverse = lax.rsqrt(jnp.mean(mixed * mixed, axis=1, keepdims=True) + norm_eps)
        normed = mixed * inverse
        cotan = cotan_ref[:, own(head)].astype(f32)
        part = jnp.sum(cotan * normed, axis=0, keepdims=True)
        own_ref[SPAN + head : SPAN + head + 1, :] = part.astype(own_ref.dtype)
        scaled = cotan * gain_ref[:, place(where, head)]
        along = jnp.mean(scaled * normed, axis=1, keepdims=True)
        grad = ((scaled - normed * along) * inverse).astype(bf16)
        grad_ref[:, own(head)] = grad
        own_ref[own(head), :] = mm_tn(query_map, grad).astype(own_ref.dtype)


def back(query_ref, key_ref, value_ref, grad_ref, state_ref, dk_ref, dv_ref, dq_ref, *_):
    length = query_ref.shape[0]
    for head in range(QUARTER):
        query = query_ref[:, own(head)].astype(f32)
        query_map = feature(query)
        key_map = feature(key_ref[:, own(head)].astype(f32))
        value = value_ref[:, own(head)]
        grad = grad_ref[:, own(head)]
        far = mm_nt(grad, state_ref[own(head), :])
        slope = decay(query)
        inside = lower(grad, value, length)
        for i, strip in enumerate(inside):
            rows = slice(i * TILE, (i + 1) * TILE)
            near = mm(strip, key_map[: (i + 1) * TILE])
            dq_ref[rows, own(head)] = ((near + far[rows]) * slope[rows]).astype(bf16)
        weights = lower(query_map, key_map, length)
        for i in range(len(inside)):
            rows, below = slice(i * TILE, (i + 1) * TILE), slice(i * TILE, length)
            column = jnp.concatenate([strip[:, rows] for strip in inside[i:]], axis=0)
            dk_ref[rows, own(head)] = mm_tn(column, query_map[below])
            column = jnp.concatenate([strip[:, rows] for strip in weights[i:]], axis=0)
            dv_ref[rows, own(head)] = mm_tn(column, grad[below])


def last_head(head, key_ref, value_ref, back_ref, dk_ref, dv_ref, key_grad_ref, value_grad_ref):
    key = key_ref[:, own(head)].astype(f32)
    back = back_ref[own(head), :]
    far = mm_nt(value_ref[:, own(head)], back)
    key_grad_ref[:, own(head)] = ((dk_ref[:, own(head)] + far) * decay(key)).astype(bf16)
    value_grad = dv_ref[:, own(head)] + mm(feature(key), back)
    value_grad_ref[:, own(head)] = value_grad.astype(bf16)


def last(key_ref, value_ref, back_ref, dk_ref, dv_ref, key_grad_ref, value_grad_ref, *_):
    for head in range(QUARTER):
        last_head(
            head, key_ref, value_ref, back_ref, dk_ref, dv_ref, key_grad_ref, value_grad_ref
        )


LAST_ORDER = ((0, 0), (1, 0), (0, 1), (1, 1))


def very_last(*refs):
    wheres, refs = [Quarter(refs[0], which) for which in LAST_ORDER], refs[1:]
    key_ref, value_ref, dk_ref, dv_ref, *backs = refs[:8]
    gain_ref, key_hbm, value_hbm, key_grad_ref, value_grad_ref, sems = refs[8:]
    for where, back_ref in zip(wheres, backs, strict=True):
        gains = back_ref[SPAN:, :].astype(f32)
        for head in range(QUARTER):
            gain_ref[:, place(where, head)] = gains[head : head + 1, :]
    copies = []
    for head in range(QUARTER):
        last_head(
            head, key_ref, value_ref, backs[0], dk_ref, dv_ref, key_grad_ref, value_grad_ref
        )
        for i, (held, whole) in enumerate(((key_grad_ref, key_hbm), (value_grad_ref, value_hbm))):
            copies.append(
                pltpu.make_async_copy(
                    held.at[:, own(head)], whole.at[:, place(wheres[0], head)], sems.at[i, head]
                )
            )
            copies[-1].start()
    finish(copies)


def call(kernel, ins, outs, scratch=(), kept=(), flops=WORK):
    return pl.pallas_call(
        kernel,
        out_shape=[jax.ShapeDtypeStruct(shape, dtype) for shape, dtype, _ in outs],
        in_specs=[spec for _, spec in ins] + [spec for _, spec, _ in kept],
        out_specs=[spec for _, _, spec in outs],
        scratch_shapes=list(scratch),
        input_output_aliases={len(ins) + i: out for i, (_, _, out) in enumerate(kept)},
        compiler_params=pltpu.CompilerParams(vmem_limit_bytes=12 << 20),
        cost_estimate=pl.CostEstimate(flops=flops, bytes_accessed=4 << 20, transcendentals=0),
    )(*[a for a, _ in ins], *[a for a, _, _ in kept])


def permute(value, pairs):
    return lax.ppermute(value, "seq", pairs)


def add(*terms):
    return functools.reduce(lambda a, b: a + b, [t.astype(f32) for t in terms])


def when(flag, wanted, value):
    value = value.astype(f32)
    return jnp.where(flag, value, 0.0) if wanted else jnp.where(flag, 0.0, value)


def after(value, *done):
    leaves, tree = jax.tree.flatten(value)
    held = lax.optimization_barrier((*leaves, *done))
    return jax.tree.unflatten(tree, held[: len(leaves)])


class Scan:
    def __init__(self, shards, reverse, odd_core, odd_chip, bits):
        self.shards = shards
        self.sign = -1 if reverse else 1
        self.second = not reverse
        self.odd_core, self.odd_chip, self.bits = odd_core, odd_chip, bits

    def swap_core(self, value):
        return permute(value, [(i, i ^ 1) for i in range(self.shards)])

    def swap_chip(self, value):
        return permute(value, [(i, i ^ 2) for i in range(self.shards)])

    def early(self, mine, got):
        self.early_mine, self.early_got = mine, got
        send = add(mine, got).astype(bf16)
        self.other = self.swap_chip(send)
        return send

    def late(self, mine, got):
        self.late_mine, self.late_got = mine, got
        self.near = add(mine, got)

    def open(self):
        self.total = add(self.near, self.other).astype(bf16)
        self.base = 0.0
        return self.total

    def exchange(self, level):
        step = 4 << level
        return permute(self.total, [(i, i ^ step) for i in range(self.shards)])

    def absorb(self, level, other):
        self.base = self.base + when(self.bits[level], self.second, other)
        self.total = add(self.total, other).astype(bf16)
        return self.total

    def alone(self, value, wanted):
        rows = lax.broadcasted_iota(jnp.int32, value.shape, 0)
        return jnp.where((rows >= SPAN) if wanted else (rows < SPAN), value, 0)

    def state(self, base, mine, got):
        if base.shape[0] > SPAN:
            mine, got = self.alone(mine, False), self.alone(got, False)
        here = add(base, when(self.odd_core, self.second, got)).astype(bf16)
        there = add(base, when(self.odd_core, not self.second, mine)).astype(bf16)
        return here, self.swap_core(there)

    def late_state(self):
        base, near, other = self.base, self.near, self.other
        if base.shape[0] > SPAN:
            base = self.alone(base, False) + self.alone(self.total, True).astype(f32)
            near, other = self.alone(near, False), self.alone(other, False)
        send = add(base, when(self.odd_chip, not self.second, near)).astype(bf16)
        self.back = self.swap_chip(send)
        base = add(base, when(self.odd_chip, self.second, other))
        return self.state(base, self.late_mine, self.late_got)

    def early_state(self):
        return self.state(self.back, self.early_mine, self.early_got)


def on_device(queries, key_vectors, value_vectors, out_cotangent, norm_gain):
    queries, key_vectors, value_vectors, out_cotangent = (
        pltpu.with_memory_space_constraint(a, pltpu.HBM)
        for a in (queries, key_vectors, value_vectors, out_cotangent)
    )
    length, width = queries.shape
    shards = lax.axis_size("seq")
    index = lax.axis_index("seq").astype(jnp.int32)
    core, chip, four = index % 2, index // 2 % 2, index // 4
    gain = norm_gain.reshape(1, width)
    levels = range((shards // 4 - 1).bit_length())
    bits = [four // (1 << level) % 2 == 1 for level in levels]
    place_in_seq, odd_core, odd_chip, bits = after(
        (index.reshape(1), core == 1, chip == 1, bits)
    )
    state_low = ((SPAN, HEAD), bf16, VMEM)
    state_wide = ((SPAN, HEAD), f32, VMEM)
    sums_low = ((SPAN + EXTRA, HEAD), bf16, VMEM)
    sums_wide = ((SPAN + EXTRA, HEAD), f32, VMEM)
    wide = ((length, SPAN), f32, VMEM)
    low = ((length, SPAN), bf16, VMEM)
    whole = ((length, width), bf16, HBM)
    row = ((1, width), f32, VMEM)
    held = lambda *arrays: [(a, VMEM) for a in arrays]
    sems = lambda *shape: pltpu.SemaphoreType.DMA(shape)
    wholes = {"q": queries, "k": key_vectors, "v": value_vectors, "c": out_cotangent}
    tile, results = {}, {}

    def moving(body, ins, outs, fetch=(), first=0, put=(), scratch=(), flops=WORK):
        names = list(dict.fromkeys(name for _, _, name in put))
        old = [(name, results[name]) for name in names if name in results]
        store_to = tuple(names.index(name) for _, _, name in put)
        counts = (
            tuple(which for _, which in fetch),
            tuple(which for which, _, _ in put),
            store_to,
            len(ins),
            len(outs),
            len(old),
            len(scratch),
            len(names),
        )
        result = call(
            functools.partial(moving_kernel, body, counts, first),
            [(place_in_seq, SMEM)]
            + ins
            + [(wholes[name], HBM) for name, _ in fetch]
            + held(*[a for _, a, _ in put]),
            outs + [low] * len(fetch) + [whole] * len(names),
            [*scratch, sems(max(1, len(fetch) + len(put)), PIECES)],
            [(a, HBM, len(outs) + len(fetch) + names.index(name)) for name, a in old],
            flops,
        )
        for key, value in zip(fetch, result[len(outs) : len(outs) + len(fetch)], strict=True):
            tile[key] = value
        for name, value in zip(names, result[len(outs) + len(fetch) :], strict=True):
            results[name] = value
        return result[: len(outs)]

    def loading(body, ins, outs, fetch=(), first=0):
        return moving(body, held(*ins), outs, fetch, first)

    def tiles(names, which):
        return [tile[name, which] for name in names]

    every = [(1, 1), (0, 1), (1, 0), (0, 0)]
    fore = Scan(shards, False, odd_core, odd_chip, bits)
    (sent,) = loading(state, [], [state_low], [(name, w) for w in every for name in "kv"], 2)
    got = fore.swap_core(sent)
    (mine,) = loading(state, after(tiles("kv", (0, 1)), sent), [state_wide])
    send = fore.early(mine, got)
    (sent,) = loading(state, after(tiles("kv", (1, 0)), send), [state_low])
    got = fore.swap_core(sent)
    (mine,) = loading(
        state, after(tiles("kv", (0, 0)), sent), [state_wide], [("q", w) for w in every]
    )
    fore.late(mine, got)

    mixed = {}
    done = fore.open()
    plan = {0: [(1, 0)], 1: [(0, 0), (0, 1), (1, 1)]}
    fetched = {(1, 0): [("c", w) for w in every]}
    for level in levels:
        moved = fore.exchange(level)
        for which in plan.get(level, []):
            (done,) = loading(
                inner, after(tiles("qkv", which), done), [wide], fetched.get(which, [])
            )
            mixed[which] = done
        done = fore.absorb(level, after(moved, done))

    grads, seen = {}, {}
    aft = Scan(shards, True, odd_core, odd_chip, bits)

    def norm(which, state, kind, *done):
        query, cotan = tiles("qc", which)
        (cotan,) = after([cotan], *done) if done else [cotan]
        ins = [(place_in_seq, SMEM)] + held(query, cotan, gain, state, mixed[which])
        return call(functools.partial(norm_kernel, which), ins, [low, kind])

    seen[0, 0], seen[1, 0] = fore.late_state()
    grads[0, 0], sent = norm((0, 0), seen[0, 0], sums_low)
    got = aft.swap_core(sent)
    grads[1, 0], mine = norm((1, 0), seen[1, 0], sums_wide)
    send = aft.early(mine, got)
    fore.back = after(fore.back, send)
    seen[0, 1], seen[1, 1] = fore.early_state()
    grads[0, 1], sent = norm((0, 1), seen[0, 1], sums_low, send)
    got = aft.swap_core(sent)
    grads[1, 1], mine = norm((1, 1), seen[1, 1], sums_wide)
    aft.late(mine, got)

    inner_grads, ready = {}, []

    def back_of(which, done, flops=WORK):
        grad = after(grads[which], done)
        *inner_grads[which], query_grad = moving(
            back, held(*tiles("qkv", which), grad, seen[which]), [wide, wide, low], flops=flops
        )
        ready.append((which, query_grad, "query"))
        return inner_grads[which][0]

    done = aft.open()
    plan = {0: [(1, 1), (0, 1)], 1: [(1, 0), (0, 0)]}
    for level in levels:
        moved = aft.exchange(level)
        for which in plan.get(level, []):
            done = back_of(which, done)
        done = aft.absorb(level, after(moved, done))

    def last_of(which, back_state):
        put = [ready.pop(0) for _ in range(len(ready))]
        key_grad, value_grad = moving(
            last,
            held(*tiles("kv", which), back_state, *inner_grads[which]),
            [low, low],
            put=put,
            flops=LIGHT,
        )
        ready.extend([(which, key_grad, "key"), (which, value_grad, "value")])
        return key_grad

    backs = {}
    backs[1, 1], backs[0, 1] = aft.late_state()
    done = last_of((1, 1), backs[1, 1])
    inner_grads[0, 1][0] = after(inner_grads[0, 1][0], done)
    done = last_of((0, 1), backs[0, 1])
    aft.back = after(aft.back, done)
    backs[1, 0], backs[0, 0] = aft.early_state()
    last_of((1, 0), backs[1, 0])
    (gain_grad,) = moving(
        very_last,
        [(place_in_seq, SMEM)]
        + held(*tiles("kv", (0, 0)), *inner_grads[0, 0], *[backs[w] for w in LAST_ORDER]),
        [row],
        put=list(ready),
        scratch=[pltpu.VMEM((length, SPAN), bf16)] * 2 + [sems(2, QUARTER)],
    )
    return results["query"], results["key"], results["value"], gain_grad.reshape(width)


def solution(mesh):
    tokens = P(("groups", "seq"), None)
    return jax.shard_map(
        on_device,
        mesh=mesh,
        in_specs=(tokens, tokens, tokens, tokens, P()),
        out_specs=(tokens, tokens, tokens, P("groups")),
        check_vma=False,
    )
```

```python
import functools

import jax
import jax.numpy as jnp
from jax import lax
from jax.experimental import pallas as pl
from jax.experimental.pallas import tpu as pltpu
from jax.sharding import PartitionSpec as P

HEADS = 16
HEAD = 128
TILE = 128
QUARTER = HEADS // 4
SPAN = QUARTER * HEAD
WORK, LIGHT = 2_000_000_000, 300_000_000
PIECES = 2
EXTRA = 16
norm_eps = 1e-05
f32 = jnp.float32
bf16 = jnp.bfloat16

VMEM = pl.BlockSpec(memory_space=pltpu.VMEM)
SMEM = pl.BlockSpec(memory_space=pltpu.SMEM)
HBM = pl.BlockSpec(memory_space=pltpu.HBM)


def decay(x):
    return jnp.exp(jnp.minimum(x, 0.0))


def feature(x):
    return jnp.where(x > 0, x + 1.0, decay(x)).astype(bf16)


def mm(a, b):
    return lax.dot_general(a, b, (((1,), (0,)), ((), ())), preferred_element_type=f32)


def mm_nt(a, b):
    return lax.dot_general(a, b, (((1,), (1,)), ((), ())), preferred_element_type=f32)


def mm_tn(a, b):
    return lax.dot_general(a, b, (((0,), (0,)), ((), ())), preferred_element_type=f32)


def own(head):
    return slice(head * HEAD, (head + 1) * HEAD)


class Quarter:
    def __init__(self, index_ref, which):
        self.index_ref, self.which = index_ref, which

    def __getitem__(self, axis):
        bit = (self.index_ref[0] >> axis) & 1
        return 1 - bit if self.which[axis] else bit


def span(where):
    return pl.ds(pl.multiple_of((2 * where[0] + where[1]) * SPAN, SPAN), SPAN)


def place(where, head):
    start = (2 * where[0] + where[1]) * SPAN + head * HEAD
    return pl.ds(pl.multiple_of(start, HEAD), HEAD)


def lower(rows, depth, length):
    keep = lax.broadcasted_iota(jnp.int32, (TILE, TILE), 0) >= lax.broadcasted_iota(
        jnp.int32, (TILE, TILE), 1
    )
    strips = []
    for start in range(0, length, TILE):
        strip = mm_nt(rows[start : start + TILE], depth[: start + TILE])
        last = jnp.where(keep, strip[:, start:], 0.0).astype(bf16)
        if start:
            last = jnp.concatenate([strip[:, :start].astype(bf16), last], axis=1)
        strips.append(last)
    return strips


def finish(copies):
    for copy in copies:
        copy.wait()


def state(key_ref, value_ref, own_ref):
    for head in range(QUARTER):
        key_map = feature(key_ref[:, own(head)].astype(f32))
        own_ref[own(head), :] = mm_tn(key_map, value_ref[:, own(head)]).astype(own_ref.dtype)


def inner(query_ref, key_ref, value_ref, mixed_ref):
    length = query_ref.shape[0]
    for head in range(QUARTER):
        query_map = feature(query_ref[:, own(head)].astype(f32))
        key_map = feature(key_ref[:, own(head)].astype(f32))
        value = value_ref[:, own(head)]
        for i, strip in enumerate(lower(query_map, key_map, length)):
            start = i * TILE
            mixed_ref[start : start + TILE, own(head)] = mm(strip, value[: start + TILE])


def chunked(source, target, sem, pieces):
    rows = source.shape[0] // pieces
    return [
        pltpu.make_async_copy(
            source.at[pl.ds(i * rows, rows)], target.at[pl.ds(i * rows, rows)], sem.at[i]
        )
        for i in range(pieces)
    ]


def moving_kernel(body, counts, first, *refs):
    load_at, store_at, store_to, body_ins, body_outs, wholes, scratch, named = counts
    loads, stores = len(load_at), len(store_to)
    refs = list(refs)

    def take(number):
        taken = refs[:number]
        del refs[:number]
        return taken

    (index_ref,) = take(1)
    load_at = [Quarter(index_ref, which) for which in load_at]
    store_at = [Quarter(index_ref, which) for which in store_at]
    ins, sources, ready = take(body_ins), take(loads), take(stores)
    take(wholes)
    outs, targets, results = take(body_outs), take(loads), take(named)
    rest, (sems,) = take(scratch), take(1)
    copies = []
    for i, (at, source, target) in enumerate(zip(load_at, sources, targets, strict=True)):
        copies.append(chunked(source.at[:, span(at)], target, sems.at[i], PIECES))
    for i, (at, source, to) in enumerate(zip(store_at, ready, store_to, strict=True)):
        target = results[to].at[:, span(at)]
        copies.append(chunked(source, target, sems.at[loads + i], PIECES))
    for copy in copies:
        for piece in copy:
            piece.start()
    for copy in copies[:first]:
        finish(copy)
    body(*targets[:first], *ins, *outs, *results, *rest)
    for copy in copies[first:]:
        finish(copy)


def norm_kernel(which, index_ref, query_ref, cotan_ref, gain_ref, state_ref, mixed_ref, grad_ref, own_ref):
    where = Quarter(index_ref, which)
    own_ref[SPAN:, :] = jnp.zeros_like(own_ref[SPAN:, :])
    for head in range(QUARTER):
        query_map = feature(query_ref[:, own(head)].astype(f32))
        mixed = mixed_ref[:, own(head)] + mm(query_map, state_ref[own(head), :])
        inverse = lax.rsqrt(jnp.mean(mixed * mixed, axis=1, keepdims=True) + norm_eps)
        normed = mixed * inverse
        cotan = cotan_ref[:, own(head)].astype(f32)
        part = jnp.sum(cotan * normed, axis=0, keepdims=True)
        own_ref[SPAN + head : SPAN + head + 1, :] = part.astype(own_ref.dtype)
        scaled = cotan * gain_ref[:, place(where, head)]
        along = jnp.mean(scaled * normed, axis=1, keepdims=True)
        grad = ((scaled - normed * along) * inverse).astype(bf16)
        grad_ref[:, own(head)] = grad
        own_ref[own(head), :] = mm_tn(query_map, grad).astype(own_ref.dtype)


def back(query_ref, key_ref, value_ref, grad_ref, state_ref, dk_ref, dv_ref, dq_ref, *_):
    length = query_ref.shape[0]
    for head in range(QUARTER):
        query = query_ref[:, own(head)].astype(f32)
        query_map = feature(query)
        key_map = feature(key_ref[:, own(head)].astype(f32))
        value = value_ref[:, own(head)]
        grad = grad_ref[:, own(head)]
        far = mm_nt(grad, state_ref[own(head), :])
        slope = decay(query)
        inside = lower(grad, value, length)
        for i, strip in enumerate(inside):
            rows = slice(i * TILE, (i + 1) * TILE)
            near = mm(strip, key_map[: (i + 1) * TILE])
            dq_ref[rows, own(head)] = ((near + far[rows]) * slope[rows]).astype(bf16)
        weights = lower(query_map, key_map, length)
        for i in range(len(inside)):
            rows, below = slice(i * TILE, (i + 1) * TILE), slice(i * TILE, length)
            column = jnp.concatenate([strip[:, rows] for strip in inside[i:]], axis=0)
            dk_ref[rows, own(head)] = mm_tn(column, query_map[below])
            column = jnp.concatenate([strip[:, rows] for strip in weights[i:]], axis=0)
            dv_ref[rows, own(head)] = mm_tn(column, grad[below])


def last_head(head, key_ref, value_ref, back_ref, dk_ref, dv_ref, key_grad_ref, value_grad_ref):
    key = key_ref[:, own(head)].astype(f32)
    back = back_ref[own(head), :]
    far = mm_nt(value_ref[:, own(head)], back)
    key_grad_ref[:, own(head)] = ((dk_ref[:, own(head)] + far) * decay(key)).astype(bf16)
    value_grad = dv_ref[:, own(head)] + mm(feature(key), back)
    value_grad_ref[:, own(head)] = value_grad.astype(bf16)


def last(key_ref, value_ref, back_ref, dk_ref, dv_ref, key_grad_ref, value_grad_ref, *_):
    for head in range(QUARTER):
        last_head(
            head, key_ref, value_ref, back_ref, dk_ref, dv_ref, key_grad_ref, value_grad_ref
        )


LAST_ORDER = ((0, 0), (1, 0), (0, 1), (1, 1))


def very_last(*refs):
    wheres, refs = [Quarter(refs[0], which) for which in LAST_ORDER], refs[1:]
    key_ref, value_ref, dk_ref, dv_ref, *backs = refs[:8]
    gain_ref, key_hbm, value_hbm, key_grad_ref, value_grad_ref, sems = refs[8:]
    copies = []
    for head in range(QUARTER):
        last_head(
            head, key_ref, value_ref, backs[0], dk_ref, dv_ref, key_grad_ref, value_grad_ref
        )
        for i, (held, whole) in enumerate(((key_grad_ref, key_hbm), (value_grad_ref, value_hbm))):
            copies.append(
                pltpu.make_async_copy(
                    held.at[:, own(head)], whole.at[:, place(wheres[0], head)], sems.at[i, head]
                )
            )
            copies[-1].start()
    for where, back_ref in zip(wheres, backs, strict=True):
        gains = back_ref[SPAN:, :].astype(f32)
        for head in range(QUARTER):
            gain_ref[:, place(where, head)] = gains[head : head + 1, :]
    finish(copies)


def call(kernel, ins, outs, scratch=(), kept=(), flops=WORK):
    return pl.pallas_call(
        kernel,
        out_shape=[jax.ShapeDtypeStruct(shape, dtype) for shape, dtype, _ in outs],
        in_specs=[spec for _, spec in ins] + [spec for _, spec, _ in kept],
        out_specs=[spec for _, _, spec in outs],
        scratch_shapes=list(scratch),
        input_output_aliases={len(ins) + i: out for i, (_, _, out) in enumerate(kept)},
        compiler_params=pltpu.CompilerParams(vmem_limit_bytes=12 << 20),
        cost_estimate=pl.CostEstimate(flops=flops, bytes_accessed=4 << 20, transcendentals=0),
    )(*[a for a, _ in ins], *[a for a, _, _ in kept])


def permute(value, pairs):
    return lax.ppermute(value, "seq", pairs)


def add(*terms):
    return functools.reduce(lambda a, b: a + b, [t.astype(f32) for t in terms])


def when(flag, wanted, value):
    value = value.astype(f32)
    return jnp.where(flag, value, 0.0) if wanted else jnp.where(flag, 0.0, value)


def after(value, *done):
    leaves, tree = jax.tree.flatten(value)
    held = lax.optimization_barrier((*leaves, *done))
    return jax.tree.unflatten(tree, held[: len(leaves)])


class Scan:
    def __init__(self, shards, reverse, odd_core, odd_chip, bits):
        self.shards = shards
        self.sign = -1 if reverse else 1
        self.second = not reverse
        self.odd_core, self.odd_chip, self.bits = odd_core, odd_chip, bits

    def swap_core(self, value):
        return permute(value, [(i, i ^ 1) for i in range(self.shards)])

    def swap_chip(self, value):
        return permute(value, [(i, i ^ 2) for i in range(self.shards)])

    def early(self, mine, got):
        self.early_mine, self.early_got = mine, got
        send = add(mine, got).astype(bf16)
        self.other = self.swap_chip(send)
        return send

    def late(self, mine, got):
        self.late_mine, self.late_got = mine, got
        self.near = add(mine, got)

    def open(self):
        self.total = add(self.near, self.other).astype(bf16)
        self.base = 0.0
        return self.total

    def exchange(self, level):
        step = 4 << level
        return permute(self.total, [(i, i ^ step) for i in range(self.shards)])

    def absorb(self, level, other):
        self.base = self.base + when(self.bits[level], self.second, other)
        self.total = add(self.total, other).astype(bf16)
        return self.total

    def alone(self, value, wanted):
        rows = lax.broadcasted_iota(jnp.int32, value.shape, 0)
        return jnp.where((rows >= SPAN) if wanted else (rows < SPAN), value, 0)

    def state(self, base, mine, got):
        if base.shape[0] > SPAN:
            mine, got = self.alone(mine, False), self.alone(got, False)
        here = add(base, when(self.odd_core, self.second, got)).astype(bf16)
        there = add(base, when(self.odd_core, not self.second, mine)).astype(bf16)
        return here, self.swap_core(there)

    def late_state(self):
        base, near, other = self.base, self.near, self.other
        if base.shape[0] > SPAN:
            base = self.alone(base, False) + self.alone(self.total, True).astype(f32)
            near, other = self.alone(near, False), self.alone(other, False)
        send = add(base, when(self.odd_chip, not self.second, near)).astype(bf16)
        self.back = self.swap_chip(send)
        base = add(base, when(self.odd_chip, self.second, other))
        return self.state(base, self.late_mine, self.late_got)

    def early_state(self):
        return self.state(self.back, self.early_mine, self.early_got)


def on_device(queries, key_vectors, value_vectors, out_cotangent, norm_gain):
    queries, key_vectors, value_vectors, out_cotangent = (
        pltpu.with_memory_space_constraint(a, pltpu.HBM)
        for a in (queries, key_vectors, value_vectors, out_cotangent)
    )
    length, width = queries.shape
    shards = lax.axis_size("seq")
    index = lax.axis_index("seq").astype(jnp.int32)
    odd = [(index >> bit) & 1 == 1 for bit in range((shards - 1).bit_length())]
    gain = norm_gain.reshape(1, width)
    levels = range((shards // 4 - 1).bit_length())
    place_in_seq, (odd_core, odd_chip, *bits) = after((index.reshape(1), odd))
    state_low = ((SPAN, HEAD), bf16, VMEM)
    state_wide = ((SPAN, HEAD), f32, VMEM)
    sums_low = ((SPAN + EXTRA, HEAD), bf16, VMEM)
    sums_wide = ((SPAN + EXTRA, HEAD), f32, VMEM)
    wide = ((length, SPAN), f32, VMEM)
    low = ((length, SPAN), bf16, VMEM)
    whole = ((length, width), bf16, HBM)
    row = ((1, width), f32, VMEM)
    held = lambda *arrays: [(a, VMEM) for a in arrays]
    sems = lambda *shape: pltpu.SemaphoreType.DMA(shape)
    wholes = {"q": queries, "k": key_vectors, "v": value_vectors, "c": out_cotangent}
    tile, results = {}, {}

    def moving(
        body, ins, outs, fetch=(), first=0, put=(), scratch=(), flops=WORK, wholes=wholes
    ):
        names = list(dict.fromkeys(name for _, _, name in put))
        old = [(name, results[name]) for name in names if name in results]
        store_to = tuple(names.index(name) for _, _, name in put)
        counts = (
            tuple(which for _, which in fetch),
            tuple(which for which, _, _ in put),
            store_to,
            len(ins),
            len(outs),
            len(old),
            len(scratch),
            len(names),
        )
        result = call(
            functools.partial(moving_kernel, body, counts, first),
            [(place_in_seq, SMEM)]
            + ins
            + [(wholes[name], HBM) for name, _ in fetch]
            + held(*[a for _, a, _ in put]),
            outs + [low] * len(fetch) + [whole] * len(names),
            [*scratch, sems(max(1, len(fetch) + len(put)), PIECES)],
            [(a, HBM, len(outs) + len(fetch) + names.index(name)) for name, a in old],
            flops,
        )
        for key, value in zip(fetch, result[len(outs) : len(outs) + len(fetch)], strict=True):
            tile[key] = value
        for name, value in zip(names, result[len(outs) + len(fetch) :], strict=True):
            results[name] = value
        return result[: len(outs)]

    def loading(body, ins, outs, fetch=(), first=0, wholes=wholes):
        return moving(body, held(*ins), outs, fetch, first, wholes=wholes)

    def fetch(names, quarters):
        return [(name, which) for which in quarters for name in names]

    def tiles(names, which):
        return [tile[name, which] for name in names]

    every = [(1, 1), (0, 1), (1, 0), (0, 0)]
    fore = Scan(shards, False, odd_core, odd_chip, bits)
    (sent,) = loading(state, [], [state_low], fetch("kv", every[:2]), 2)
    got = fore.swap_core(sent)
    (mine,) = loading(state, after(tiles("kv", (0, 1)), sent), [state_wide])
    send = fore.early(mine, got)
    late = after(wholes, send)
    (sent,) = loading(state, [], [state_low], fetch("kv", every[2:]), 2, late)
    got = fore.swap_core(sent)
    (mine,) = loading(state, after(tiles("kv", (0, 0)), sent), [state_wide])
    fore.late(mine, got)

    mixed = {}
    done = fore.open()
    plan = {0: [(1, 0)], 1: [(0, 0), (0, 1), (1, 1)]}
    fetched = {(1, 0): fetch("q", every[2:] + every[:2]), (0, 0): fetch("c", every)}
    for level in levels:
        moved = fore.exchange(level)
        for which in plan.get(level, []):
            first = 0 if ("q", which) in tile else 1
            ins = after(tiles("qkv"[first:], which), done)
            (done,) = loading(inner, ins, [wide], fetched.get(which, []), first)
            mixed[which] = done
        done = fore.absorb(level, after(moved, done))

    grads, seen = {}, {}
    aft = Scan(shards, True, odd_core, odd_chip, bits)

    def norm(which, state, kind, *done):
        query, cotan = tiles("qc", which)
        (cotan,) = after([cotan], *done) if done else [cotan]
        ins = [(place_in_seq, SMEM)] + held(query, cotan, gain, state, mixed[which])
        return call(functools.partial(norm_kernel, which), ins, [low, kind])

    seen[0, 0], seen[1, 0] = fore.late_state()
    grads[0, 0], sent = norm((0, 0), seen[0, 0], sums_low)
    got = aft.swap_core(sent)
    grads[1, 0], mine = norm((1, 0), seen[1, 0], sums_wide)
    send = aft.early(mine, got)
    fore.back = after(fore.back, send)
    seen[0, 1], seen[1, 1] = fore.early_state()
    grads[0, 1], sent = norm((0, 1), seen[0, 1], sums_low, send)
    got = aft.swap_core(sent)
    grads[1, 1], mine = norm((1, 1), seen[1, 1], sums_wide)
    aft.late(mine, got)

    inner_grads, ready = {}, []

    def back_of(which, done, flops=WORK):
        grad = after(grads[which], done)
        *inner_grads[which], query_grad = moving(
            back, held(*tiles("qkv", which), grad, seen[which]), [wide, wide, low], flops=flops
        )
        ready.append((which, query_grad, "query"))
        return inner_grads[which][0]

    done = aft.open()
    plan = {0: [(1, 1), (0, 1)], 1: [(1, 0), (0, 0)]}
    for level in levels:
        moved = aft.exchange(level)
        for which in plan.get(level, []):
            done = back_of(which, done)
        done = aft.absorb(level, after(moved, done))

    def last_of(which, back_state):
        put = [ready.pop(0) for _ in range(len(ready))]
        key_grad, value_grad = moving(
            last,
            held(*tiles("kv", which), back_state, *inner_grads[which]),
            [low, low],
            put=put,
            flops=LIGHT,
        )
        ready.extend([(which, key_grad, "key"), (which, value_grad, "value")])
        return key_grad

    backs = {}
    backs[1, 1], backs[0, 1] = aft.late_state()
    done = last_of((1, 1), backs[1, 1])
    inner_grads[0, 1][0] = after(inner_grads[0, 1][0], done)
    done = last_of((0, 1), backs[0, 1])
    aft.back = after(aft.back, done)
    backs[1, 0], backs[0, 0] = aft.early_state()
    last_of((1, 0), backs[1, 0])
    (gain_grad,) = moving(
        very_last,
        [(place_in_seq, SMEM)]
        + held(*tiles("kv", (0, 0)), *inner_grads[0, 0], *[backs[w] for w in LAST_ORDER]),
        [row],
        put=list(ready),
        scratch=[pltpu.VMEM((length, SPAN), bf16)] * 2 + [sems(2, QUARTER)],
    )
    return results["query"], results["key"], results["value"], gain_grad.reshape(width)


def solution(mesh):
    tokens = P(("groups", "seq"), None)
    return jax.shard_map(
        on_device,
        mesh=mesh,
        in_specs=(tokens, tokens, tokens, tokens, P()),
        out_specs=(tokens, tokens, tokens, P("groups")),
        check_vma=False,
    )
```

```python
import functools

import jax
import jax.numpy as jnp
from jax import lax
from jax.experimental import pallas as pl
from jax.experimental.pallas import tpu as pltpu
from jax.sharding import PartitionSpec as P

HEADS = 16
HEAD = 128
TILE = 128
QUARTER = HEADS // 4
SPAN = QUARTER * HEAD
WORK = 2_000_000_000
PIECES = 2
EXTRA = 16
norm_eps = 1e-05
f32 = jnp.float32
bf16 = jnp.bfloat16

VMEM = pl.BlockSpec(memory_space=pltpu.VMEM)
SMEM = pl.BlockSpec(memory_space=pltpu.SMEM)
HBM = pl.BlockSpec(memory_space=pltpu.HBM)


def decay(x):
    return jnp.exp(jnp.minimum(x, 0.0))


def feature(x):
    return jnp.where(x > 0, x + 1.0, decay(x)).astype(bf16)


def mm(a, b):
    return lax.dot_general(a, b, (((1,), (0,)), ((), ())), preferred_element_type=f32)


def mm_nt(a, b):
    return lax.dot_general(a, b, (((1,), (1,)), ((), ())), preferred_element_type=f32)


def mm_tn(a, b):
    return lax.dot_general(a, b, (((0,), (0,)), ((), ())), preferred_element_type=f32)


def own(head):
    return slice(head * HEAD, (head + 1) * HEAD)


class Quarter:
    def __init__(self, index_ref, which):
        self.index_ref, self.which = index_ref, which

    def __getitem__(self, axis):
        bit = (self.index_ref[0] >> axis) & 1
        return 1 - bit if self.which[axis] else bit


def span(where):
    return pl.ds(pl.multiple_of((2 * where[0] + where[1]) * SPAN, SPAN), SPAN)


def place(where, head):
    start = (2 * where[0] + where[1]) * SPAN + head * HEAD
    return pl.ds(pl.multiple_of(start, HEAD), HEAD)


def lower(rows, depth, length):
    keep = lax.broadcasted_iota(jnp.int32, (TILE, TILE), 0) >= lax.broadcasted_iota(
        jnp.int32, (TILE, TILE), 1
    )
    strips = []
    for start in range(0, length, TILE):
        strip = mm_nt(rows[start : start + TILE], depth[: start + TILE])
        last = jnp.where(keep, strip[:, start:], 0.0).astype(bf16)
        if start:
            last = jnp.concatenate([strip[:, :start].astype(bf16), last], axis=1)
        strips.append(last)
    return strips


def finish(copies):
    for copy in copies:
        copy.wait()


def state(key_ref, value_ref, own_ref):
    for head in range(QUARTER):
        key_map = feature(key_ref[:, own(head)].astype(f32))
        own_ref[own(head), :] = mm_tn(key_map, value_ref[:, own(head)]).astype(own_ref.dtype)


def inner(query_ref, key_ref, value_ref, mixed_ref):
    length = query_ref.shape[0]
    for head in range(QUARTER):
        query_map = feature(query_ref[:, own(head)].astype(f32))
        key_map = feature(key_ref[:, own(head)].astype(f32))
        value = value_ref[:, own(head)]
        for i, strip in enumerate(lower(query_map, key_map, length)):
            start = i * TILE
            mixed_ref[start : start + TILE, own(head)] = mm(strip, value[: start + TILE])


def chunked(source, target, sem, pieces):
    rows = source.shape[0] // pieces
    return [
        pltpu.make_async_copy(
            source.at[pl.ds(i * rows, rows)], target.at[pl.ds(i * rows, rows)], sem.at[i]
        )
        for i in range(pieces)
    ]


def moving_kernel(body, counts, first, *refs):
    load_at, store_at, store_to, body_ins, body_outs, wholes, scratch, named = counts
    loads, stores = len(load_at), len(store_to)
    refs = list(refs)

    def take(number):
        taken = refs[:number]
        del refs[:number]
        return taken

    (index_ref,) = take(1)
    load_at = [Quarter(index_ref, which) for which in load_at]
    store_at = [Quarter(index_ref, which) for which in store_at]
    ins, sources, ready = take(body_ins), take(loads), take(stores)
    take(wholes)
    outs, targets, results = take(body_outs), take(loads), take(named)
    rest, (sems,) = take(scratch), take(1)
    copies = []
    for i, (at, source, target) in enumerate(zip(load_at, sources, targets, strict=True)):
        copies.append(chunked(source.at[:, span(at)], target, sems.at[i], PIECES))
    for i, (at, source, to) in enumerate(zip(store_at, ready, store_to, strict=True)):
        target = results[to].at[:, span(at)]
        copies.append(chunked(source, target, sems.at[loads + i], PIECES))
    for copy in copies:
        for piece in copy:
            piece.start()
    for copy in copies[:first]:
        finish(copy)
    body(*targets[:first], *ins, *outs, *results, *rest)
    for copy in copies[first:]:
        finish(copy)


def norm_kernel(which, index_ref, query_ref, cotan_ref, gain_ref, state_ref, mixed_ref, grad_ref, own_ref):
    where = Quarter(index_ref, which)
    own_ref[SPAN:, :] = jnp.zeros_like(own_ref[SPAN:, :])
    for head in range(QUARTER):
        query_map = feature(query_ref[:, own(head)].astype(f32))
        mixed = mixed_ref[:, own(head)] + mm(query_map, state_ref[own(head), :])
        inverse = lax.rsqrt(jnp.mean(mixed * mixed, axis=1, keepdims=True) + norm_eps)
        normed = mixed * inverse
        cotan = cotan_ref[:, own(head)].astype(f32)
        part = jnp.sum(cotan * normed, axis=0, keepdims=True)
        own_ref[SPAN + head : SPAN + head + 1, :] = part.astype(own_ref.dtype)
        scaled = cotan * gain_ref[:, place(where, head)]
        along = jnp.mean(scaled * normed, axis=1, keepdims=True)
        grad = ((scaled - normed * along) * inverse).astype(bf16)
        grad_ref[:, own(head)] = grad
        own_ref[own(head), :] = mm_tn(query_map, grad).astype(own_ref.dtype)


def back(query_ref, key_ref, value_ref, grad_ref, state_ref, dk_ref, dv_ref, dq_ref, *_):
    length = query_ref.shape[0]
    for head in range(QUARTER):
        query = query_ref[:, own(head)].astype(f32)
        query_map = feature(query)
        key_map = feature(key_ref[:, own(head)].astype(f32))
        value = value_ref[:, own(head)]
        grad = grad_ref[:, own(head)]
        far = mm_nt(grad, state_ref[own(head), :])
        slope = decay(query)
        inside = lower(grad, value, length)
        for i, strip in enumerate(inside):
            rows = slice(i * TILE, (i + 1) * TILE)
            near = mm(strip, key_map[: (i + 1) * TILE])
            dq_ref[rows, own(head)] = ((near + far[rows]) * slope[rows]).astype(bf16)
        weights = lower(query_map, key_map, length)
        for i in range(len(inside)):
            rows, below = slice(i * TILE, (i + 1) * TILE), slice(i * TILE, length)
            column = jnp.concatenate([strip[:, rows] for strip in inside[i:]], axis=0)
            dk_ref[rows, own(head)] = mm_tn(column, query_map[below])
            column = jnp.concatenate([strip[:, rows] for strip in weights[i:]], axis=0)
            dv_ref[rows, own(head)] = mm_tn(column, grad[below])


def last_head(head, key_ref, value_ref, back_ref, dk_ref, dv_ref, key_grad_ref, value_grad_ref):
    key = key_ref[:, own(head)].astype(f32)
    back = back_ref[own(head), :]
    far = mm_nt(value_ref[:, own(head)], back)
    key_grad_ref[:, own(head)] = ((dk_ref[:, own(head)] + far) * decay(key)).astype(bf16)
    value_grad = dv_ref[:, own(head)] + mm(feature(key), back)
    value_grad_ref[:, own(head)] = value_grad.astype(bf16)


def last(key_ref, value_ref, back_ref, dk_ref, dv_ref, key_grad_ref, value_grad_ref, *_):
    for head in range(QUARTER):
        last_head(
            head, key_ref, value_ref, back_ref, dk_ref, dv_ref, key_grad_ref, value_grad_ref
        )


LAST_ORDER = ((0, 0), (1, 0), (0, 1), (1, 1))


def very_last(*refs):
    wheres, refs = [Quarter(refs[0], which) for which in LAST_ORDER], refs[1:]
    key_ref, value_ref, dk_ref, dv_ref, *backs = refs[:8]
    gain_ref, key_hbm, value_hbm, key_grad_ref, value_grad_ref, sems = refs[8:]
    copies = []
    for head in range(QUARTER):
        last_head(
            head, key_ref, value_ref, backs[0], dk_ref, dv_ref, key_grad_ref, value_grad_ref
        )
        for i, (held, whole) in enumerate(((key_grad_ref, key_hbm), (value_grad_ref, value_hbm))):
            copies.append(
                pltpu.make_async_copy(
                    held.at[:, own(head)], whole.at[:, place(wheres[0], head)], sems.at[i, head]
                )
            )
            copies[-1].start()
    for where, back_ref in zip(wheres, backs, strict=True):
        gains = back_ref[SPAN:, :].astype(f32)
        for head in range(QUARTER):
            gain_ref[:, place(where, head)] = gains[head : head + 1, :]
    finish(copies)


def call(kernel, ins, outs, scratch=(), kept=(), flops=WORK):
    return pl.pallas_call(
        kernel,
        out_shape=[jax.ShapeDtypeStruct(shape, dtype) for shape, dtype, _ in outs],
        in_specs=[spec for _, spec in ins] + [spec for _, spec, _ in kept],
        out_specs=[spec for _, _, spec in outs],
        scratch_shapes=list(scratch),
        input_output_aliases={len(ins) + i: out for i, (_, _, out) in enumerate(kept)},
        compiler_params=pltpu.CompilerParams(vmem_limit_bytes=12 << 20),
        cost_estimate=pl.CostEstimate(flops=flops, bytes_accessed=4 << 20, transcendentals=0),
    )(*[a for a, _ in ins], *[a for a, _, _ in kept])


def permute(value, pairs):
    return lax.ppermute(value, "seq", pairs)


def add(*terms):
    return functools.reduce(lambda a, b: a + b, [t.astype(f32) for t in terms])


def when(flag, wanted, value):
    value = value.astype(f32)
    return jnp.where(flag, value, 0.0) if wanted else jnp.where(flag, 0.0, value)


def after(value, *done):
    leaves, tree = jax.tree.flatten(value)
    held = lax.optimization_barrier((*leaves, *done))
    return jax.tree.unflatten(tree, held[: len(leaves)])


class Scan:
    def __init__(self, shards, reverse, odd_core, odd_chip, bits):
        self.shards = shards
        self.sign = -1 if reverse else 1
        self.second = not reverse
        self.odd_core, self.odd_chip, self.bits = odd_core, odd_chip, bits

    def swap_core(self, value):
        return permute(value, [(i, i ^ 1) for i in range(self.shards)])

    def swap_chip(self, value):
        return permute(value, [(i, i ^ 2) for i in range(self.shards)])

    def early(self, mine, got):
        self.early_mine, self.early_got = mine, got
        send = add(mine, got).astype(bf16)
        self.other = self.swap_chip(send)
        return send

    def late(self, mine, got):
        self.late_mine, self.late_got = mine, got
        self.near = add(mine, got)

    def open(self):
        self.total = add(self.near, self.other).astype(bf16)
        self.base = 0.0
        return self.total

    def exchange(self, level):
        step = 4 << level
        return permute(self.total, [(i, i ^ step) for i in range(self.shards)])

    def absorb(self, level, other):
        self.base = self.base + when(self.bits[level], self.second, other)
        self.total = add(self.total, other).astype(bf16)
        return self.total

    def alone(self, value, wanted):
        rows = lax.broadcasted_iota(jnp.int32, value.shape, 0)
        return jnp.where((rows >= SPAN) if wanted else (rows < SPAN), value, 0)

    def state(self, base, mine, got):
        if base.shape[0] > SPAN:
            mine, got = self.alone(mine, False), self.alone(got, False)
        here = add(base, when(self.odd_core, self.second, got)).astype(bf16)
        there = add(base, when(self.odd_core, not self.second, mine)).astype(bf16)
        return here, self.swap_core(there)

    def late_state(self):
        base, near, other = self.base, self.near, self.other
        if base.shape[0] > SPAN:
            base = self.alone(base, False) + self.alone(self.total, True).astype(f32)
            near, other = self.alone(near, False), self.alone(other, False)
        send = add(base, when(self.odd_chip, not self.second, near)).astype(bf16)
        self.back = self.swap_chip(send)
        base = add(base, when(self.odd_chip, self.second, other))
        return self.state(base, self.late_mine, self.late_got)

    def early_state(self):
        return self.state(self.back, self.early_mine, self.early_got)


def on_device(queries, key_vectors, value_vectors, out_cotangent, norm_gain):
    queries, key_vectors, value_vectors, out_cotangent = (
        pltpu.with_memory_space_constraint(a, pltpu.HBM)
        for a in (queries, key_vectors, value_vectors, out_cotangent)
    )
    length, width = queries.shape
    shards = lax.axis_size("seq")
    index = lax.axis_index("seq").astype(jnp.int32)
    odd = [(index >> bit) & 1 == 1 for bit in range((shards - 1).bit_length())]
    gain = norm_gain.reshape(1, width)
    levels = range((shards // 4 - 1).bit_length())
    place_in_seq, (odd_core, odd_chip, *bits) = after((index.reshape(1), odd))
    state_low = ((SPAN, HEAD), bf16, VMEM)
    state_wide = ((SPAN, HEAD), f32, VMEM)
    sums_low = ((SPAN + EXTRA, HEAD), bf16, VMEM)
    sums_wide = ((SPAN + EXTRA, HEAD), f32, VMEM)
    wide = ((length, SPAN), f32, VMEM)
    low = ((length, SPAN), bf16, VMEM)
    whole = ((length, width), bf16, HBM)
    row = ((1, width), f32, VMEM)
    held = lambda *arrays: [(a, VMEM) for a in arrays]
    sems = lambda *shape: pltpu.SemaphoreType.DMA(shape)
    wholes = {"q": queries, "k": key_vectors, "v": value_vectors, "c": out_cotangent}
    tile, results = {}, {}

    def moving(
        body, ins, outs, fetch=(), first=0, put=(), scratch=(), flops=WORK, wholes=wholes
    ):
        names = list(dict.fromkeys(name for _, _, name in put))
        old = [(name, results[name]) for name in names if name in results]
        store_to = tuple(names.index(name) for _, _, name in put)
        counts = (
            tuple(which for _, which in fetch),
            tuple(which for which, _, _ in put),
            store_to,
            len(ins),
            len(outs),
            len(old),
            len(scratch),
            len(names),
        )
        result = call(
            functools.partial(moving_kernel, body, counts, first),
            [(place_in_seq, SMEM)]
            + ins
            + [(wholes[name], HBM) for name, _ in fetch]
            + held(*[a for _, a, _ in put]),
            outs + [low] * len(fetch) + [whole] * len(names),
            [*scratch, sems(max(1, len(fetch) + len(put)), PIECES)],
            [(a, HBM, len(outs) + len(fetch) + names.index(name)) for name, a in old],
            flops,
        )
        for key, value in zip(fetch, result[len(outs) : len(outs) + len(fetch)], strict=True):
            tile[key] = value
        for name, value in zip(names, result[len(outs) + len(fetch) :], strict=True):
            results[name] = value
        return result[: len(outs)]

    def loading(body, ins, outs, fetch=(), first=0, wholes=wholes):
        return moving(body, held(*ins), outs, fetch, first, wholes=wholes)

    def fetch(names, quarters):
        return [(name, which) for which in quarters for name in names]

    def tiles(names, which):
        return [tile[name, which] for name in names]

    every = [(1, 1), (0, 1), (1, 0), (0, 0)]
    fore = Scan(shards, False, odd_core, odd_chip, bits)
    (sent,) = loading(state, [], [state_low], fetch("kv", every[:2]), 2)
    got = fore.swap_core(sent)
    (mine,) = loading(state, after(tiles("kv", (0, 1)), sent), [state_wide])
    send = fore.early(mine, got)
    late = after(wholes, send)
    (sent,) = loading(state, [], [state_low], fetch("kv", every[2:]), 2, late)
    got = fore.swap_core(sent)
    (mine,) = loading(state, after(tiles("kv", (0, 0)), sent), [state_wide])
    fore.late(mine, got)

    mixed = {}
    done = fore.open()
    plan = {0: [(1, 0)], 1: [(0, 0), (0, 1), (1, 1)]}
    fetched = {(1, 0): fetch("q", every[2:] + every[:2]), (0, 0): fetch("c", every)}
    for level in levels:
        moved = fore.exchange(level)
        for which in plan.get(level, []):
            first = 0 if ("q", which) in tile else 1
            ins = after(tiles("qkv"[first:], which), done)
            (done,) = loading(inner, ins, [wide], fetched.get(which, []), first)
            mixed[which] = done
        done = fore.absorb(level, after(moved, done))

    grads, seen = {}, {}
    aft = Scan(shards, True, odd_core, odd_chip, bits)

    def norm(which, state, kind, *done):
        query, cotan = tiles("qc", which)
        (cotan,) = after([cotan], *done) if done else [cotan]
        ins = [(place_in_seq, SMEM)] + held(query, cotan, gain, state, mixed[which])
        return call(functools.partial(norm_kernel, which), ins, [low, kind])

    seen[0, 0], seen[1, 0] = fore.late_state()
    grads[0, 0], sent = norm((0, 0), seen[0, 0], sums_low)
    got = aft.swap_core(sent)
    grads[1, 0], mine = norm((1, 0), seen[1, 0], sums_wide)
    send = aft.early(mine, got)
    fore.back = after(fore.back, send)
    seen[0, 1], seen[1, 1] = fore.early_state()
    grads[0, 1], sent = norm((0, 1), seen[0, 1], sums_low, send)
    got = aft.swap_core(sent)
    grads[1, 1], mine = norm((1, 1), seen[1, 1], sums_wide)
    aft.late(mine, got)

    inner_grads, ready = {}, []

    def back_of(which, done, flops=WORK):
        grad = after(grads[which], done)
        *inner_grads[which], query_grad = moving(
            back, held(*tiles("qkv", which), grad, seen[which]), [wide, wide, low], flops=flops
        )
        ready.append((which, query_grad, "query"))
        return inner_grads[which][0]

    done = aft.open()
    plan = {0: [(1, 1), (0, 1)], 1: [(1, 0), (0, 0)]}
    for level in levels:
        moved = aft.exchange(level)
        for which in plan.get(level, []):
            done = back_of(which, done)
        done = aft.absorb(level, after(moved, done))

    def last_of(which, back_state):
        put = [ready.pop(0) for _ in range(len(ready))]
        key_grad, value_grad = moving(
            last,
            held(*tiles("kv", which), back_state, *inner_grads[which]),
            [low, low],
            put=put,
        )
        ready.extend([(which, key_grad, "key"), (which, value_grad, "value")])
        return key_grad

    backs = {}
    backs[1, 1], backs[0, 1] = aft.late_state()
    done = last_of((1, 1), backs[1, 1])
    inner_grads[0, 1][0] = after(inner_grads[0, 1][0], done)
    done = last_of((0, 1), backs[0, 1])
    aft.back = after(aft.back, done)
    backs[1, 0], backs[0, 0] = aft.early_state()
    last_of((1, 0), backs[1, 0])
    (gain_grad,) = moving(
        very_last,
        [(place_in_seq, SMEM)]
        + held(*tiles("kv", (0, 0)), *inner_grads[0, 0], *[backs[w] for w in LAST_ORDER]),
        [row],
        put=list(ready),
        scratch=[pltpu.VMEM((length, SPAN), bf16)] * 2 + [sems(2, QUARTER)],
    )
    return results["query"], results["key"], results["value"], gain_grad.reshape(width)


def solution(mesh):
    tokens = P(("groups", "seq"), None)
    return jax.shard_map(
        on_device,
        mesh=mesh,
        in_specs=(tokens, tokens, tokens, tokens, P()),
        out_specs=(tokens, tokens, tokens, P("groups")),
        check_vma=False,
    )
```
